256 devices in a mesh: pipe: 4 (over y), tensor: 32 (over x, z_hi, core), dp: 2 (over z_lo).
Axes of the slice: x: 4, y: 4, z: 8 (z_hi: 4, z_lo: 2; z = z_hi * 2 + z_lo), core: 2. Of those that a mesh axis runs over, the one named last changes fastest.
Arguments:
- weight_main: bfloat16 [4, 4096, 2, 8192], P('pipe', None, None, 'tensor'), may hold values from -0.09375 to 0.09375
- weight_state: bfloat16 [4, 4096, 2, 1024], P('pipe', None, None, 'tensor'), may hold values from -0.09375 to 0.09375
- weight_step: bfloat16 [4, 128, 4096], P('pipe', 'tensor'), may hold values from -0.09375 to 0.09375
- weight_out: bfloat16 [4, 8192, 4096], P('pipe', 'tensor'), may hold values from -0.0625 to 0.0625
- conv_main: float32 [4, 4, 8192], P('pipe', None, 'tensor'), may hold values from -3 to 3
- conv_state: float32 [4, 4, 2, 1024], P('pipe'), may hold values from -3 to 3
- step_bias: float32 [4, 128], P('pipe', 'tensor'), may hold values from -3 to 0
- decay_log: float32 [4, 128], P('pipe', 'tensor'), may hold values from -5 to 0.5
- skip_gain: float32 [4, 128], P('pipe', 'tensor'), may hold values from 1 to 6
- norm_gain: float32 [4, 8192], P('pipe', 'tensor'), may hold values from 0.5 to 1.5
- saved_main: bfloat16 [4, 256, 2, 8192], P('pipe', 'dp', None, 'tensor'), parts along dimension 1, may hold values from -6 to 6
- saved_state: bfloat16 [4, 256, 2, 1024], P('pipe', 'dp'), parts along dimension 1, may hold values from -6 to 6
- saved_step: bfloat16 [4, 128, 256], P('pipe', 'tensor', 'dp'), parts along dimension 2, may hold values from -6 to 6
- output_grad: bfloat16 [256, 4096], P('dp', 'tensor'), parts along dimension 0, may hold values from -6 to 6
Outputs:
- input_grads: bfloat16 [4, 256, 4096], P('pipe', 'dp', 'tensor'), parts along dimension 1
The draws below stay inside these ranges and needn't reach their ends.
There are 2 independent parts, one for each index of `dp`. The reference program is written for one: setup_inputs(seed, part) draws one part's arguments, and reference() takes and returns one part's arrays. A program takes and returns all parts, laid end to end along the dimension named above; an argument that names none is the same for every part. Nothing has to cross between parts.
All inputs are finite; a program needn't handle non-finite values.
Results may differ from the reference program's by a relative error of at most 0.02.
Values may be sent and summed in bfloat16 or wider, within the bound.
A program may use at most 64 MiB of HBM per device.

```python
import jax
import jax.numpy as jnp
from jax import lax

D = 4096
HEADS_DEV = 4
HEAD_DIM = 64
NSTATE = 128
GROUP_SPAN = 4
KCONV = 4
STRETCH = 128
SEQLEN = 128
HEADS = 128
GROUPS = 8
N_PIPE = 4


def level_of(stream_key, shape, pieces, smallest, top_value):
    def one(dim, shards_of):
        draws = jax.random.uniform(jax.random.fold_in(jax.random.fold_in(stream_key, 6), dim), (shards_of,), jnp.float32, smallest / len(pieces), top_value / len(pieces))
        return jnp.repeat(jnp.exp(draws), shape[dim] // shards_of).reshape((-1,) + (1,) * (len(shape) - dim - 1))

    factor_of = one(*pieces[0])
    for cut in pieces[1:]:
        factor_of = factor_of * one(*cut)
    return factor_of


def gaussian(own_key, shape, width, limit, shards=(), held_as=jnp.bfloat16):
    entries = jax.random.normal(own_key, shape, jnp.float32) * width
    if len(shards) > 0:
        entries = level_of(own_key, shape, shards, -0.22, 0.18) * entries
    return jnp.clip(entries, min=-limit, max=limit).astype(held_as)


def setup_inputs(seed: int = 0, part: int = 0) -> dict:
    keys = jax.random.split(jax.random.key(seed), 15)
    part_keys = jax.random.split(jax.random.fold_in(keys[14], part), 15)
    weight_main = gaussian(keys[0], (N_PIPE, D, 2, HEADS * HEAD_DIM), D ** -0.5, 0.09375, ((0, 4), (3, 32)))
    weight_state = gaussian(keys[1], (N_PIPE, D, 2, GROUPS * NSTATE), D ** -0.5, 0.09375, ((0, 4), (3, 32)))
    weight_step = gaussian(keys[2], (N_PIPE, HEADS, D), D ** -0.5, 0.09375, ((0, 4), (1, 32)))
    weight_out = gaussian(keys[3], (N_PIPE, HEADS * HEAD_DIM, D), (HEADS * HEAD_DIM) ** -0.5, 0.0625, ((0, 4), (1, 32)))
    conv_main = gaussian(keys[4], (N_PIPE, KCONV, HEADS * HEAD_DIM), KCONV ** -0.5, 3.0, ((0, 4), (2, 32)), jnp.float32)
    conv_state = gaussian(keys[5], (N_PIPE, KCONV, 2, GROUPS * NSTATE), KCONV ** -0.5, 3.0, ((0, 4),), jnp.float32)
    step_bias = jnp.clip(-3.0 + 3.0 * jax.random.uniform(keys[6], (N_PIPE, HEADS), jnp.float32) ** level_of(keys[6], (N_PIPE, HEADS), ((0, 4), (1, 32)), -0.2, 0.2), -3.0, 0.0)
    decay_log = jnp.clip(-5.0 + 5.5 * jax.random.uniform(keys[7], (N_PIPE, HEADS), jnp.float32) ** level_of(keys[7], (N_PIPE, HEADS), ((0, 4), (1, 32)), -0.2, 0.2), -5.0, 0.5)
    skip_gain = jnp.clip(1.0 + 5.0 * jax.random.uniform(keys[8], (N_PIPE, HEADS), jnp.float32) ** level_of(keys[8], (N_PIPE, HEADS), ((0, 4), (1, 32)), -0.2, 0.2), 1.0, 6.0)
    norm_gain = jnp.clip(0.5 + 1.0 * jax.random.uniform(keys[9], (N_PIPE, HEADS * HEAD_DIM), jnp.float32) ** level_of(keys[9], (N_PIPE, HEADS * HEAD_DIM), ((0, 4), (1, 32)), -0.2, 0.2), 0.5, 1.5)
    saved_main = gaussian(part_keys[10], (N_PIPE, SEQLEN, 2, HEADS * HEAD_DIM), 1.0, 6.0, ((0, 4), (3, 32)))
    saved_state = gaussian(part_keys[11], (N_PIPE, SEQLEN, 2, GROUPS * NSTATE), 1.0, 6.0, ((0, 4),))
    saved_step = gaussian(part_keys[12], (N_PIPE, HEADS, SEQLEN), 1.0, 6.0, ((0, 4), (1, 32)))
    output_grad = gaussian(part_keys[13], (SEQLEN, D), 1.0, 6.0, ((1, 32),))
    return {"weight_main": weight_main, "weight_state": weight_state, "weight_step": weight_step, "weight_out": weight_out, "conv_main": conv_main, "conv_state": conv_state, "step_bias": step_bias, "decay_log": decay_log, "skip_gain": skip_gain, "norm_gain": norm_gain, "saved_main": saved_main, "saved_state": saved_state, "saved_step": saved_step, "output_grad": output_grad}


EPSILON = 1e-05
HIGHEST = lax.Precision.HIGHEST

def causal_conv(signal, kernel):
    taps = kernel.shape[0]
    length = signal.shape[0]
    padded = jnp.pad(signal, ((taps - 1, 0), (0, 0)))
    summed = kernel[0] * padded[0:length]
    for offset in range(1, taps):
        summed = summed + kernel[offset] * padded[offset:offset + length]
    return summed

def state_space(values, step_sizes, decay_rates, inputs, readout):
    length, head_count, head_size = values.shape
    blocks = length // STRETCH
    state_width = inputs.shape[1]
    decays = (step_sizes * decay_rates[:, None]).reshape(head_count, blocks, STRETCH)
    running = jnp.cumsum(decays, axis=2)
    scaled = (values * step_sizes.T[:, :, None]).reshape(blocks, STRETCH, head_count, head_size)
    inputs_blocked = inputs.reshape(blocks, STRETCH, state_width)
    readout_blocked = readout.reshape(blocks, STRETCH, state_width)
    scores = jnp.einsum('cin,cjn->cij', readout_blocked, inputs_blocked, precision=HIGHEST)
    position = jnp.arange(STRETCH)
    causal = position[:, None] >= position[None, :]
    differ = running[:, :, :, None] - running[:, :, None, :]
    weights = jnp.where(causal, jnp.exp(jnp.where(causal, differ, 0.0)), 0.0) * scores[None]
    within = jnp.einsum('hcij,cjhp->cihp', weights, scaled, precision=HIGHEST)
    tail_decay = jnp.exp(running[:, :, -1:] - running)
    weighted = scaled * jnp.transpose(tail_decay, (1, 2, 0))[:, :, :, None]
    block_sums = jnp.einsum('cjhp,cjn->chpn', weighted, inputs_blocked, precision=HIGHEST)
    shrinks = jnp.exp(running[:, :, -1]).T

    def advance(carried, item):
        newest, shrink = item
        return (carried * shrink[:, None, None] + newest, carried)
    anchor = jnp.zeros((head_count, head_size, state_width), jnp.float32)
    _, entering = lax.scan(advance, anchor, (block_sums, shrinks))
    across = jnp.einsum('cin,chpn->cihp', readout_blocked, entering, precision=HIGHEST)
    across = across * jnp.transpose(jnp.exp(running), (1, 2, 0))[:, :, :, None]
    return (within + across).reshape(length, head_count, head_size)

def mamba_mixer(main_proj, state_proj, step_proj, conv_main, conv_state, step_bias, decay_log, skip_gain, norm_gain):
    length = main_proj.shape[0]
    head_count = step_proj.shape[0]
    gating = main_proj[:, 0]
    mixed_in = jax.nn.silu(causal_conv(main_proj[:, 1], conv_main))
    flat_state = state_proj.reshape(length, -1)
    state_conv = jax.nn.silu(causal_conv(flat_state, conv_state.reshape(conv_state.shape[0], -1))).reshape(length, 2, -1)
    step_sizes = jax.nn.softplus(step_proj + step_bias[:, None])
    decay_rates = -jnp.exp(decay_log)
    values = mixed_in.reshape(length, head_count, -1)
    scanned = state_space(values, step_sizes, decay_rates, state_conv[:, 0], state_conv[:, 1])
    scanned = scanned + skip_gain[None, :, None] * values
    gated = scanned.reshape(length, -1) * jax.nn.silu(gating)
    inverse = lax.rsqrt(lax.optimization_barrier(jnp.mean(gated * gated, axis=1, keepdims=True)) + EPSILON)
    return gated * inverse * norm_gain

def reference(weight_main, weight_state, weight_step, weight_out, conv_main, conv_state, step_bias, decay_log, skip_gain, norm_gain, saved_main, saved_state, saved_step, output_grad):
    group_width = HEADS_DEV * HEAD_DIM
    quarter = NSTATE // GROUP_SPAN
    carry = output_grad
    results = []
    for section in range(N_PIPE - 1, -1, -1):

        def group_term(summed, group):
            state_start = (group * NSTATE).astype(jnp.int32)
            state_part = lax.dynamic_slice_in_dim(saved_state[section], state_start, NSTATE, 2).astype(jnp.float32)
            conv_state_part = lax.dynamic_slice_in_dim(conv_state[section], state_start, NSTATE, 2)

            def member_term(state_total, member):
                device = group * GROUP_SPAN + member
                channel_start = (device * group_width).astype(jnp.int32)
                head_start = (device * HEADS_DEV).astype(jnp.int32)
                main_part = lax.dynamic_slice_in_dim(saved_main[section], channel_start, group_width, 2).astype(jnp.float32)
                step_part = lax.dynamic_slice_in_dim(saved_step[section], head_start, HEADS_DEV, 0).astype(jnp.float32)
                conv_main_part = lax.dynamic_slice_in_dim(conv_main[section], channel_start, group_width, 1)
                bias_part = lax.dynamic_slice_in_dim(step_bias[section], head_start, HEADS_DEV, 0)
                decay_part = lax.dynamic_slice_in_dim(decay_log[section], head_start, HEADS_DEV, 0)
                skip_part = lax.dynamic_slice_in_dim(skip_gain[section], head_start, HEADS_DEV, 0)
                gain_part = lax.dynamic_slice_in_dim(norm_gain[section], channel_start, group_width, 0)
                out_rows = lax.dynamic_slice_in_dim(weight_out[section], channel_start, group_width, 0)
                main_cols = lax.dynamic_slice_in_dim(weight_main[section], channel_start, group_width, 2).reshape(D, -1)
                step_rows = lax.dynamic_slice_in_dim(weight_step[section], head_start, HEADS_DEV, 0)

                def local_mixer(first_in, second_in, third_in):
                    return mamba_mixer(first_in, second_in, third_in, conv_main_part, conv_state_part, bias_part, decay_part, skip_part, gain_part)
                dnormed = lax.dot_general(carry, out_rows, (((1,), (1,)), ((), ())), preferred_element_type=jnp.float32)
                _, pullback = jax.vjp(local_mixer, main_part, state_part, step_part)
                grad_main, grad_state, grad_step = pullback(dnormed)
                grad_main = grad_main.astype(jnp.bfloat16).reshape(SEQLEN, -1)
                grad_step = grad_step.astype(jnp.bfloat16)
                partial_sum = lax.dot_general(grad_main, main_cols, (((1,), (1,)), ((), ())), preferred_element_type=jnp.float32)
                partial_sum = partial_sum + lax.dot_general(grad_step, step_rows, (((0,), (0,)), ((), ())), preferred_element_type=jnp.float32)
                return (state_total + grad_state, partial_sum)
            anchor = jnp.zeros((SEQLEN, 2, NSTATE), jnp.float32)
            state_total, partials = lax.scan(member_term, anchor, jnp.arange(GROUP_SPAN, dtype=jnp.int32))
            grad_state = state_total.astype(jnp.bfloat16)
            for member in range(GROUP_SPAN):
                piece = grad_state[:, :, member * quarter:(member + 1) * quarter].reshape(SEQLEN, -1)
                cols = lax.dynamic_slice_in_dim(weight_state[section], state_start + member * quarter, quarter, 2).reshape(D, -1)
                term = partials[member] + lax.dot_general(piece, cols, (((1,), (1,)), ((), ())), preferred_element_type=jnp.float32)
                summed = summed + term
            return (summed, None)
        summed, _ = lax.scan(group_term, jnp.zeros((SEQLEN, D), jnp.float32), jnp.arange(GROUPS, dtype=jnp.int32))
        carry = summed.astype(jnp.bfloat16)
        results.append(carry)
    return jnp.stack(results[::-1])
```

```python
import jax
import jax.numpy as jnp
from jax import lax
from jax.experimental import pallas as pl
from jax.experimental.pallas import tpu as pltpu
from jax.sharding import PartitionSpec as P

F32 = jnp.float32
BF16 = jnp.bfloat16
HIGHEST = lax.Precision.HIGHEST
EPSILON = 1e-05
MESH = pl.DeviceIdType.MESH
NX = 4
NZ = 4
T = 128
FAR = (2, 1, 3, 0)


def nn(a, b, precision=None):
    return lax.dot_general(
        a, b, (((1,), (0,)), ((), ())), preferred_element_type=F32, precision=precision
    )


def nt(a, b, precision=None):
    return lax.dot_general(
        a, b, (((1,), (1,)), ((), ())), preferred_element_type=F32, precision=precision
    )


def shift_down(v, n, rows):
    if n == 0:
        return v
    return jnp.where(rows >= n, pltpu.roll(v, n, 0), 0.0)


def shift_up(v, n, rows):
    if n == 0:
        return v
    return jnp.where(rows < T - n, pltpu.roll(v, T - n, 0), 0.0)


def conv(v, taps, rows):
    out = taps[3:4] * v
    for k in range(3):
        out = out + taps[k : k + 1] * shift_down(v, 3 - k, rows)
    return out


def conv_back(v, taps, rows):
    out = taps[3:4] * v
    for k in range(3):
        out = out + taps[k : k + 1] * shift_up(v, 3 - k, rows)
    return out


def kernel(
    wm_hbm, ws_hbm, wt_hbm, wo_hbm,
    main_ref, state_ref, stepin_ref, vec_ref, cm_ref, cs_ref, gain_ref, og_ref,
    out_ref,
    WM, WO, WS, G, Q, PS, PR, RS, RR, XS, XR, ZS, ZR,
    NRM, SGI, YSP, MIX, STL, DSM, DSS, EM, SC, WTC, SCM, BC, SIG, L1, L2,
    wsem, ssem, rsem,
):
    s = lax.axis_index("pipe")
    t = lax.axis_index("tensor")
    x = t // 8
    z = (t // 2) % 4
    c = t % 2
    right_x = (x + 1) % NX
    left_x = (x + 3) % NX
    below = (s + 3) % 4
    above = (s + 1) % 4

    def place(px, pz, pc):
        return (px * NZ + pz) * 2 + pc

    def dev(tt, ss=None):
        if ss is None:
            return {"tensor": tt}
        return {"pipe": ss, "tensor": tt}

    count = [0]
    pending = []

    def remote(src, dst, target):
        i = count[0]
        count[0] += 1
        return pltpu.make_async_remote_copy(
            src_ref=src, dst_ref=dst, send_sem=ssem.at[i], recv_sem=rsem.at[i],
            device_id=target, device_id_type=MESH,
        )

    def go(copy):
        copy.start()
        pending.append(copy)
        return copy

    mate = dev(place(x, z, 1 - c))
    to_right = dev(place(right_x, z, c))
    to_left = dev(place(left_x, z, c))
    pair_z = z + 1 - 2 * (z % 2)
    to_pair = dev(place(x, pair_z, c))

    barrier = pltpu.get_barrier_semaphore()
    partners = [mate, to_right, to_left]
    for o in (1, 2, 3):
        partners.append(dev(place(x, (z + o) % NZ, c)))
    for o in range(4):
        partners.append(dev(place(x, (z + o) % NZ, c), below))
        partners.append(dev(place(x, (z + o) % NZ, c), above))
    for p in partners:
        pl.semaphore_signal(barrier, inc=1, device_id=p, device_id_type=MESH)

    m = t % 4
    loads = [
        pltpu.make_async_copy(wo_hbm.at[:, pl.ds(i * 256, 256)], WO.at[i], wsem.at[i])
        for i in range(16)
    ]
    loads.append(pltpu.make_async_copy(wm_hbm, WM, wsem.at[16]))
    own_b = pl.multiple_of(m * 32, 32)
    own_c = pl.multiple_of(128 + m * 32, 32)
    loads.append(pltpu.make_async_copy(ws_hbm.at[0], WS.at[pl.ds(own_b, 32)], wsem.at[17]))
    loads.append(pltpu.make_async_copy(ws_hbm.at[1], WS.at[pl.ds(own_c, 32)], wsem.at[18]))
    loads.append(pltpu.make_async_copy(wt_hbm, WS.at[256:384], wsem.at[19]))
    for load in loads:
        load.start()

    pl.semaphore_wait(barrier, len(partners))

    def hand_off(block, ids):
        copies = []
        for n, o in enumerate(FAR):
            slot = (4 - o) % 4
            copies.append(
                pltpu.make_async_remote_copy(
                    src_ref=block, dst_ref=G.at[c, 0, slot],
                    send_sem=ssem.at[ids[n]], recv_sem=rsem.at[ids[n]],
                    device_id=dev(place(x, (z + o) % NZ, c), below), device_id_type=MESH,
                )
            )
        return copies

    hand_ids = []
    for _ in range(4):
        hand_ids.append(count[0])
        count[0] += 1

    first = hand_off(og_ref, hand_ids)

    @pl.when(s == 0)
    def _():
        for copy in first:
            copy.start()

    mine = [
        remote(ws_hbm.at[0], WS.at[pl.ds(own_b, 32)], mate),
        remote(ws_hbm.at[1], WS.at[pl.ds(own_c, 32)], mate),
        remote(ws_hbm.at[0], WS.at[pl.ds(own_b, 32)], to_pair),
        remote(ws_hbm.at[1], WS.at[pl.ds(own_c, 32)], to_pair),
    ]
    for copy in mine:
        go(copy)
    far_b = pl.multiple_of(((m + 2) % 4) * 32, 32)
    far_c = pl.multiple_of(128 + ((m + 2) % 4) * 32, 32)
    passed = [
        remote(WS.at[pl.ds(far_b, 32)], WS.at[pl.ds(far_b, 32)], mate),
        remote(WS.at[pl.ds(far_c, 32)], WS.at[pl.ds(far_c, 32)], mate),
    ]

    rows = lax.broadcasted_iota(jnp.int32, (T, 256), 0)
    ri = lax.broadcasted_iota(jnp.int32, (T, T), 0)
    ci = lax.broadcasted_iota(jnp.int32, (T, T), 1)
    causal = ri >= ci
    rep = (
        lax.broadcasted_iota(jnp.int32, (T, 256), 0)
        == lax.broadcasted_iota(jnp.int32, (T, 256), 1) // 64
    ).astype(F32)
    gate = main_ref[:, 0:256].astype(F32)
    cm = cm_ref[...]
    cs = cs_ref[...]
    mixed = conv(main_ref[:, 256:512].astype(F32), cm, rows)
    sig = jax.nn.sigmoid(mixed)
    mix = mixed * sig
    DSM[...] = sig * (1.0 + mixed * (1.0 - sig))
    MIX[...] = mix
    states = conv(state_ref[...].astype(F32), cs, rows)
    sig = jax.nn.sigmoid(states)
    DSS[...] = sig * (1.0 + states * (1.0 - sig))
    states = states * sig
    BC[...] = states.astype(BF16)
    scores = nt(states[:, 128:256], states[:, 0:128], HIGHEST)
    SC[...] = scores
    vec = vec_ref[...]
    raw = stepin_ref[...] + vec[0:1]
    SIG[...] = jax.nn.sigmoid(raw)
    step = jnp.maximum(raw, 0.0) + jnp.log1p(jnp.exp(-jnp.abs(raw)))
    rate = -jnp.exp(vec[1:2])
    run_col = nn(causal.astype(F32), step * rate, HIGHEST)
    run_row = run_col.T
    stepl = nn(step, rep, HIGHEST)
    STL[...] = stepl
    skipl = nn(vec, rep, HIGHEST)[2:3]
    scaled = mix * stepl
    lane = lax.broadcasted_iota(jnp.int32, (T, T), 1)
    low = lane < 64
    ys = []
    for pair in range(2):
        sp = scaled[:, pair * 128 : pair * 128 + 128]
        acc = None
        for half in range(2):
            h = pair * 2 + half
            differ = run_col[:, h : h + 1] - run_row[h : h + 1, :]
            em = jnp.where(causal, jnp.exp(jnp.where(causal, differ, 0.0)), 0.0)
            EM[h] = em
            w = em * scores
            WTC[pair, :, half * 128 : half * 128 + 128] = w.T.astype(BF16)
            keep = low if half == 0 else jnp.logical_not(low)
            sh = jnp.where(keep, sp, 0.0)
            SCM[h] = sh.astype(BF16)
            part = nn(w, sh, HIGHEST)
            acc = part if acc is None else acc + part
        ys.append(acc)
    y = jnp.concatenate(ys, axis=1) + skipl * mix
    sg = jax.nn.sigmoid(gate)
    silu_gate = gate * sg
    gated = y * silu_gate
    inverse = lax.rsqrt(jnp.sum(gated * gated, axis=1, keepdims=True) * (1.0 / 256.0) + EPSILON)
    NRM[...] = gated * inverse
    SGI[...] = silu_gate * inverse
    YSP[...] = y * (sg * (1.0 + gate * (1.0 - sg))) * inverse

    ks = (0, 1, 3, 2)
    halves = (pl.ds(0, 64), pl.ds(64, 64))
    to_r = [remote(G.at[c, 0, k], G.at[c, 3, k], to_right) for k in range(4)]
    to_l = [remote(G.at[c, 0, k], G.at[c, 1, k], to_left) for k in range(4)]
    rel_r = [remote(G.at[c, 3, k, halves[0]], G.at[c, 2, k, halves[0]], to_right) for k in range(4)]
    rel_l = [remote(G.at[c, 1, k, halves[1]], G.at[c, 2, k, halves[1]], to_left) for k in range(4)]
    to_m = [[remote(G.at[c, j, k], G.at[c, j, k], mate) for k in range(4)] for j in range(4)]
    arrive = {}
    for n, o in enumerate(FAR):
        arrive[(4 - o) % 4] = first[n]

    for k in ks:
        arrive[k].wait_recv()
        go(to_r[k])
        go(to_l[k])
        go(to_m[0][k])
    for k in ks:
        to_r[k].wait_recv()
        go(rel_r[k])
        go(to_m[3][k])
        to_l[k].wait_recv()
        go(rel_l[k])
        go(to_m[1][k])
    for i in range(16):
        loads[i].wait()
    acc = None
    for j in (0, 3, 1, 2):
        for k in ks:
            if j == 2:
                rel_r[k].wait_recv()
                rel_l[k].wait_recv()
                go(to_m[2][k])
    for j in (0, 3, 1, 2):
        for k in ks:
            to_m[j][k].wait_recv()
            index = ((x + j) % NX) * NZ + (z + k) % NZ
            block = jnp.concatenate([G[0, j, k], G[1, j, k]], axis=1)
            part = nt(block, WO[index])
            acc = part if acc is None else acc + part

    dn = acc * gain_ref[...]
    nrm = NRM[...]
    mu = jnp.sum(dn * nrm, axis=1, keepdims=True) * (1.0 / 256.0)
    e = dn - nrm * mu
    dy = e * SGI[...]
    L1[:, 0:256] = (e * YSP[...]).astype(BF16)
    dyb = dy.astype(BF16)
    dscs = []
    ds = None
    masks = []
    for pair in range(2):
        dyp = dyb[:, pair * 128 : pair * 128 + 128]
        zero = jnp.zeros_like(dyp)
        both = jnp.concatenate([jnp.where(low, dyp, zero), jnp.where(low, zero, dyp)], axis=0)
        dscs.append(nn(WTC[pair], both))
        for half in range(2):
            h = pair * 2 + half
            a = nt(dyp, SCM[h]) * EM[h]
            ds = a if ds is None else ds + a
            masks.append((a * SC[...]).astype(BF16))
    dscaled = jnp.concatenate(dscs, axis=1)
    upper = (ci >= ri).astype(BF16)
    sums = nn(upper, jnp.concatenate(masks, axis=1))
    before = jnp.concatenate([ci < ri] * 4, axis=1)
    sums = jnp.where(before, sums, 0.0).astype(BF16)
    pick = (
        lax.broadcasted_iota(jnp.int32, (512, T), 0) // 128
        == lax.broadcasted_iota(jnp.int32, (512, T), 1)
    ).astype(BF16)
    ddecay = nn(sums, pick)
    pick64 = (
        lax.broadcasted_iota(jnp.int32, (256, T), 0) // 64
        == lax.broadcasted_iota(jnp.int32, (256, T), 1)
    ).astype(BF16)
    dstep = nn((dscaled * MIX[...]).astype(BF16), pick64)
    vec = vec_ref[...]
    dstep = dstep + ddecay * -jnp.exp(vec[1:2])
    L2[:, 256:384] = (dstep * SIG[...]).astype(BF16)
    skipl = nn(vec, rep, HIGHEST)[2:3]
    dmix = (dscaled * STL[...] + skipl * dy) * DSM[...]
    L1[:, 256:512] = conv_back(dmix, cm_ref[...], rows).astype(BF16)
    dsb = ds.astype(BF16)
    db = nn(ds.T.astype(BF16), BC[:, 128:256])
    dc = nn(dsb, BC[:, 0:128])
    dstate = jnp.concatenate([db, dc], axis=1) * DSS[...]
    L2[:, 0:256] = conv_back(dstate, cs_ref[...], rows).astype(BF16)

    mine[2].wait_recv()
    mine[3].wait_recv()
    for copy in passed:
        go(copy)
    mine[0].wait_recv()
    mine[1].wait_recv()
    for copy in passed:
        copy.wait_recv()
    for i in range(16, 20):
        loads[i].wait()

    lhs1 = L1[...]
    lhs2 = L2[...]
    first_core = c == 0
    to_mate = {}
    for j in FAR:
        for k in range(4):
            index = ((x + j) % NX) * NZ + (z + FAR[k]) % NZ
            at = pl.multiple_of(index * 256, 256)
            part = nt(lhs1, WM[pl.ds(at, 256), :]) + nn(lhs2, WS[:, pl.ds(at, 256)])
            lower, upper_half = part[:, 0:128], part[:, 128:256]
            Q[j, k] = jnp.where(first_core, lower, upper_half)
            PS[j, k] = jnp.where(first_core, upper_half, lower).astype(BF16)
            to_mate[j, k] = go(remote(PS.at[j, k], PR.at[j, k], mate))

    def chip_sum(j, k):
        to_mate[j, k].wait_recv()
        return Q[j, k] + PR[j, k].astype(F32)

    relays = {}
    for k in range(4):
        RS[k] = chip_sum(2, k).astype(BF16)
        relays[k] = go(remote(RS.at[k], RR.at[k], to_right if k % 2 == 0 else to_left))
    sends = {}

    def send_side(side, k, merged):
        value = chip_sum(1 if side == 0 else 3, k)
        if merged:
            relays[k].wait_recv()
            value = value + RR[k].astype(F32)
        XS[side, k] = value.astype(BF16)
        sends[side, k] = go(remote(XS.at[side, k], XR.at[side, k], to_right if side == 0 else to_left))

    for k in range(4):
        send_side(1 - k % 2, k, False) if k % 2 == 0 else send_side(0, k, False)
    for k in range(4):
        send_side(0 if k % 2 == 0 else 1, k, True)
    total = None
    zcopies = []
    for k in range(4):
        value = chip_sum(0, k)
        for side in range(2):
            sends[side, k].wait_recv()
            value = value + XR[side, k].astype(F32)
        if k < 3:
            ZS[k] = value.astype(BF16)
            zcopies.append(
                go(remote(ZS.at[k], ZR.at[k], dev(place(x, (z + FAR[k]) % NZ, c))))
            )
        else:
            total = value
    for k in (1, 2, 0):
        zcopies[k].wait_recv()
        total = total + ZR[k].astype(F32)
    out_ref[...] = total.astype(BF16)

    last = hand_off(out_ref, hand_ids)

    @pl.when(s > 0)
    def _():
        for copy in last:
            copy.start()

    for copy in last:
        copy.wait_send()
    for copy in pending:
        copy.wait_send()


N_COPIES = 4 + 4 + 2 + 16 + 16 + 16 + 4 + 8 + 3


def body(
    weight_main, weight_state, weight_step, weight_out, conv_main, conv_state, step_bias,
    decay_log, skip_gain, norm_gain, saved_main, saved_state, saved_step, output_grad,
):
    group = lax.axis_index("tensor") // 4
    wm = weight_main[0].reshape(4096, 512)
    ws = jnp.transpose(weight_state[0], (1, 2, 0))
    wt = jnp.pad(weight_step[0], ((0, 124), (0, 0)))
    main = saved_main[0].reshape(T, 512)
    state = lax.dynamic_slice_in_dim(saved_state[0], group * 128, 128, 2).reshape(T, 256)
    cs = lax.dynamic_slice_in_dim(conv_state[0], group * 128, 128, 2).reshape(4, 256)
    stepin = jnp.pad(saved_step[0].astype(F32).T, ((0, 0), (0, 124)))
    vec = jnp.pad(
        jnp.concatenate([step_bias, decay_log, skip_gain], axis=0), ((0, 5), (0, 124))
    )
    vmem = pl.BlockSpec(memory_space=pltpu.VMEM)
    hbm = pl.BlockSpec(memory_space=pl.ANY)
    block = (T, T)
    wide = (T, 256)
    result = pl.pallas_call(
        kernel,
        out_shape=jax.ShapeDtypeStruct((T, T), BF16),
        in_specs=[hbm] * 4 + [vmem] * 8,
        out_specs=vmem,
        scratch_shapes=[
            pltpu.VMEM((4096, 512), BF16),
            pltpu.VMEM((16, 256, 256), BF16),
            pltpu.VMEM((384, 4096), BF16),
            pltpu.VMEM((2, 4, 4) + block, BF16),
            pltpu.VMEM((4, 4) + block, F32),
            pltpu.VMEM((4, 4) + block, BF16),
            pltpu.VMEM((4, 4) + block, BF16),
            pltpu.VMEM((4,) + block, BF16),
            pltpu.VMEM((4,) + block, BF16),
            pltpu.VMEM((2, 4) + block, BF16),
            pltpu.VMEM((2, 4) + block, BF16),
            pltpu.VMEM((3,) + block, BF16),
            pltpu.VMEM((3,) + block, BF16),
            pltpu.VMEM(wide, F32),
            pltpu.VMEM(wide, F32),
            pltpu.VMEM(wide, F32),
            pltpu.VMEM(wide, F32),
            pltpu.VMEM(wide, F32),
            pltpu.VMEM(wide, F32),
            pltpu.VMEM(wide, F32),
            pltpu.VMEM((4,) + block, F32),
            pltpu.VMEM(block, F32),
            pltpu.VMEM((2, T, 256), BF16),
            pltpu.VMEM((4,) + block, BF16),
            pltpu.VMEM(wide, BF16),
            pltpu.VMEM(block, F32),
            pltpu.VMEM((T, 512), BF16),
            pltpu.VMEM((T, 384), BF16),
            pltpu.SemaphoreType.DMA((20,)),
            pltpu.SemaphoreType.DMA((N_COPIES + 16,)),
            pltpu.SemaphoreType.DMA((N_COPIES + 16,)),
        ],
        compiler_params=pltpu.CompilerParams(
            collective_id=0, has_side_effects=True, vmem_limit_bytes=48 * 1024 * 1024
        ),
        name="relay",
    )(wm, ws, wt, weight_out[0], main, state, stepin, vec, conv_main[0], cs, norm_gain, output_grad)
    return result[None]


def solution(mesh):
    return jax.shard_map(
        body,
        mesh=mesh,
        in_specs=(
            P("pipe", None, None, "tensor"),
            P("pipe", None, None, "tensor"),
            P("pipe", "tensor", None),
            P("pipe", "tensor", None),
            P("pipe", None, "tensor"),
            P("pipe", None, None, None),
            P("pipe", "tensor"),
            P("pipe", "tensor"),
            P("pipe", "tensor"),
            P("pipe", "tensor"),
            P("pipe", "dp", None, "tensor"),
            P("pipe", "dp", None, None),
            P("pipe", "tensor", "dp"),
            P("dp", "tensor"),
        ),
        out_specs=P("pipe", "dp", "tensor"),
        check_vma=False,
    )
```

```python
import jax
import jax.numpy as jnp
from jax import lax
from jax.experimental import pallas as pl
from jax.experimental.pallas import tpu as pltpu
from jax.sharding import PartitionSpec as P

F32 = jnp.float32
BF16 = jnp.bfloat16
HIGHEST = lax.Precision.HIGHEST
EPSILON = 1e-05
MESH = pl.DeviceIdType.MESH
NX = 4
NZ = 4
T = 128
FAR = (2, 1, 3, 0)
H = 1
TH = T // H


def nn(a, b, precision=None):
    return lax.dot_general(
        a, b, (((1,), (0,)), ((), ())), preferred_element_type=F32, precision=precision
    )


def nt(a, b, precision=None):
    return lax.dot_general(
        a, b, (((1,), (1,)), ((), ())), preferred_element_type=F32, precision=precision
    )


def shift_down(v, n, rows):
    if n == 0:
        return v
    return jnp.where(rows >= n, pltpu.roll(v, n, 0), 0.0)


def shift_up(v, n, rows):
    if n == 0:
        return v
    return jnp.where(rows < T - n, pltpu.roll(v, T - n, 0), 0.0)


def conv(v, taps, rows):
    out = taps[3:4] * v
    for k in range(3):
        out = out + taps[k : k + 1] * shift_down(v, 3 - k, rows)
    return out


def conv_back(v, taps, rows):
    out = taps[3:4] * v
    for k in range(3):
        out = out + taps[k : k + 1] * shift_up(v, 3 - k, rows)
    return out


def kernel(
    wm_hbm, ws_hbm, wo_hbm,
    wt_ref, main_ref, state_ref, stepin_ref, vec_ref, cm_ref, cs_ref, gain_ref, og_ref,
    out_ref,
    WM, WO, WS, G, Q, PS, PR, XS, XR, ZS, ZR,
    NRM, SGI, YSP, MIX, STL, DSM, DSS, EM, SC, WTC, SCM, BC, SIG, SK, L1, L2, AS, AR, PM,
    wsem, ssem, rsem,
):
    s = lax.axis_index("pipe")
    t = lax.axis_index("tensor")
    x = t // 8
    z = (t // 2) % 4
    c = t % 2
    right_x = (x + 1) % NX
    left_x = (x + 3) % NX
    below = (s + 3) % 4
    above = (s + 1) % 4

    def place(px, pz, pc):
        return (px * NZ + pz) * 2 + pc

    def dev(tt, ss=None):
        if ss is None:
            return {"tensor": tt}
        return {"pipe": ss, "tensor": tt}

    count = [0]
    pending = []

    def remote(src, dst, target):
        i = count[0]
        count[0] += 1
        return pltpu.make_async_remote_copy(
            src_ref=src, dst_ref=dst, send_sem=ssem.at[i], recv_sem=rsem.at[i],
            device_id=target, device_id_type=MESH,
        )

    def go(copy):
        copy.start()
        pending.append(copy)
        return copy

    mate = dev(place(x, z, 1 - c))
    to_right = dev(place(right_x, z, c))
    to_left = dev(place(left_x, z, c))
    to_opposite = dev(place((x + 2) % NX, z, c))
    pair_z = z + 1 - 2 * (z % 2)
    to_pair = dev(place(x, pair_z, c))

    barrier = pltpu.get_barrier_semaphore()
    partners = [mate, to_right, to_left, to_opposite]
    for o in (1, 2, 3):
        partners.append(dev(place(x, (z + o) % NZ, c)))
    for o in range(4):
        partners.append(dev(place(x, (z + o) % NZ, c), below))
        partners.append(dev(place(x, (z + o) % NZ, c), above))
    for p in partners:
        pl.semaphore_signal(barrier, inc=1, device_id=p, device_id_type=MESH)

    loads = [
        pltpu.make_async_copy(wo_hbm.at[:, pl.ds(i * 256, 256)], WO.at[i], wsem.at[i])
        for i in range(16)
    ]
    loads.append(pltpu.make_async_copy(wm_hbm, WM, wsem.at[16]))
    own_b = pl.ds(pl.multiple_of(c * 32, 32), 32)
    own_c = pl.ds(pl.multiple_of(64 + c * 32, 32), 32)
    loads.append(pltpu.make_async_copy(ws_hbm.at[0], WS.at[own_b], wsem.at[17]))
    loads.append(pltpu.make_async_copy(ws_hbm.at[1], WS.at[own_c], wsem.at[18]))
    for load in loads:
        load.start()

    pl.semaphore_wait(barrier, len(partners))

    pieces = [pl.ds(h * TH, TH) for h in range(H)]
    hand_ids = list(range(count[0], count[0] + 4 * H))
    count[0] += 4 * H

    def hand_off(block, h):
        copies = []
        for n, o in enumerate(FAR):
            i = hand_ids[4 * h + n]
            copies.append(
                pltpu.make_async_remote_copy(
                    src_ref=block.at[pieces[h]], dst_ref=G.at[c, 0, (4 - o) % 4, pieces[h]],
                    send_sem=ssem.at[i], recv_sem=rsem.at[i],
                    device_id=dev(place(x, (z + o) % NZ, c), below), device_id_type=MESH,
                )
            )
        return copies

    first = [hand_off(og_ref, h) for h in range(H)]

    @pl.when(s == 0)
    def _():
        for copies in first:
            for copy in copies:
                copy.start()

    mine = [
        go(remote(ws_hbm.at[0], WS.at[own_b], mate)),
        go(remote(ws_hbm.at[1], WS.at[own_c], mate)),
    ]
    WS[128:256, :] = jnp.zeros((128, 4096), BF16)
    WS[128:132, :] = wt_ref[...]

    rows = lax.broadcasted_iota(jnp.int32, (T, 256), 0)
    ri = lax.broadcasted_iota(jnp.int32, (T, T), 0)
    ci = lax.broadcasted_iota(jnp.int32, (T, T), 1)
    causal = ri >= ci
    rep = (
        lax.broadcasted_iota(jnp.int32, (T, 256), 0)
        == lax.broadcasted_iota(jnp.int32, (T, 256), 1) // 64
    ).astype(F32)
    gate = main_ref[:, 0:256].astype(F32)
    cm = cm_ref[...]
    cs = cs_ref[...]
    mixed = conv(main_ref[:, 256:512].astype(F32), cm, rows)
    sig = jax.nn.sigmoid(mixed)
    mix = mixed * sig
    DSM[...] = sig * (1.0 + mixed * (1.0 - sig))
    MIX[...] = mix
    states = conv(state_ref[...].astype(F32), cs, rows)
    sig = jax.nn.sigmoid(states)
    DSS[...] = sig * (1.0 + states * (1.0 - sig))
    states = states * sig
    BC[...] = states.astype(BF16)
    scores = nt(states[:, 128:256], states[:, 0:128], HIGHEST)
    SC[...] = scores
    vec = vec_ref[...]
    raw = stepin_ref[...] + vec[0:1]
    SIG[...] = jax.nn.sigmoid(raw)
    step = jnp.maximum(raw, 0.0) + jnp.log1p(jnp.exp(-jnp.abs(raw)))
    rate = -jnp.exp(vec[1:2])
    run_col = nn(causal.astype(F32), step * rate, HIGHEST)
    run_row = run_col.T
    stepl = nn(step, rep, HIGHEST)
    STL[...] = stepl
    SK[...] = nn(vec, rep, HIGHEST)
    skipl = SK[2:3]
    scaled = mix * stepl
    low = ci < 64
    ys = []
    for pair in range(2):
        sp = scaled[:, pair * 128 : pair * 128 + 128]
        acc = None
        for half in range(2):
            h = pair * 2 + half
            differ = run_col[:, h : h + 1] - run_row[h : h + 1, :]
            em = jnp.where(causal, jnp.exp(jnp.where(causal, differ, 0.0)), 0.0)
            EM[h] = em
            w = em * scores
            WTC[pair, :, half * 128 : half * 128 + 128] = w.T.astype(BF16)
            keep = low if half == 0 else jnp.logical_not(low)
            sh = jnp.where(keep, sp, 0.0)
            SCM[h] = sh.astype(BF16)
            part = nn(w, sh, HIGHEST)
            acc = part if acc is None else acc + part
        ys.append(acc)
    y = jnp.concatenate(ys, axis=1) + skipl * mix
    sg = jax.nn.sigmoid(gate)
    silu_gate = gate * sg
    gated = y * silu_gate
    inverse = lax.rsqrt(jnp.sum(gated * gated, axis=1, keepdims=True) * (1.0 / 256.0) + EPSILON)
    NRM[...] = gated * inverse
    SGI[...] = silu_gate * inverse
    YSP[...] = y * (sg * (1.0 + gate * (1.0 - sg))) * inverse

    ks = (0, 1, 3, 2)

    def spread(src_j, dst_j, target, h, k):
        return remote(G.at[c, src_j, k, pieces[h]], G.at[c, dst_j, k, pieces[h]], target)

    grid = [(h, k) for h in range(H) for k in ks]
    to_r = {hk: spread(0, 3, to_right, *hk) for hk in grid}
    to_l = {hk: spread(0, 1, to_left, *hk) for hk in grid}
    to_o = {hk: spread(0, 2, to_opposite, *hk) for hk in grid}
    to_m = {(j, h, k): spread(j, j, mate, h, k) for j in range(4) for h, k in grid}

    for h, k in grid:
        first[h][FAR.index((4 - k) % 4)].wait_recv()
        go(to_o[h, k])
        go(to_r[h, k])
        go(to_l[h, k])
        go(to_m[0, h, k])
    for h, k in grid:
        to_r[h, k].wait_recv()
        go(to_m[3, h, k])
        to_l[h, k].wait_recv()
        go(to_m[1, h, k])
    for i in range(16):
        loads[i].wait()
    totals = [None]

    def multiply(j):
        for k in ks:
            for h in range(H):
                to_m[j, h, k].wait_recv()
            index = ((x + j) % NX) * NZ + (z + k) % NZ
            block = jnp.concatenate([G[0, j, k], G[1, j, k]], axis=1)
            part = nt(block, WO[index])
            totals[0] = part if totals[0] is None else totals[0] + part

    multiply(0)
    multiply(3)
    for h, k in grid:
        to_o[h, k].wait_recv()
        go(to_m[2, h, k])
    multiply(1)
    multiply(2)
    acc = totals[0]

    dn = acc * gain_ref[...]
    nrm = NRM[...]
    mu = jnp.sum(dn * nrm, axis=1, keepdims=True) * (1.0 / 256.0)
    e = dn - nrm * mu
    dy = e * SGI[...]
    L1[:, 0:256] = (e * YSP[...]).astype(BF16)
    dyb = dy.astype(BF16)
    ds = None
    masks = []
    for h in range(4):
        a = nt(dyb[:, h // 2 * 128 : h // 2 * 128 + 128], SCM[h]) * EM[h]
        ds = a if ds is None else ds + a
        masks.append((a * SC[...]).astype(BF16))
    db = nn(ds.T.astype(BF16), BC[:, 128:256])
    dc = nn(ds.astype(BF16), BC[:, 0:128])
    dstate = conv_back(jnp.concatenate([db, dc], axis=1) * DSS[...], cs_ref[...], rows)
    db, dc = dstate[:, 0:128], dstate[:, 128:256]
    near = jnp.where(low, db, pltpu.roll(dc, 64, 1))
    far = jnp.where(low, pltpu.roll(db, 64, 1), dc)
    even = z % 2 == 0
    own_state = jnp.where(even, near, far)
    AS[...] = jnp.where(even, far, near).astype(BF16)
    swap = go(remote(AS, AR, to_pair))
    dscs = []
    for pair in range(2):
        dyp = dyb[:, pair * 128 : pair * 128 + 128]
        zero = jnp.zeros_like(dyp)
        both = jnp.concatenate([jnp.where(low, dyp, zero), jnp.where(low, zero, dyp)], axis=0)
        dscs.append(nn(WTC[pair], both))
    dscaled = jnp.concatenate(dscs, axis=1)
    dmix = (dscaled * STL[...] + SK[2:3] * dy) * DSM[...]
    L1[:, 256:512] = conv_back(dmix, cm_ref[...], rows).astype(BF16)
    upper = (ci >= ri).astype(BF16)
    sums = nn(upper, jnp.concatenate(masks, axis=1))
    before = jnp.concatenate([ci < ri] * 4, axis=1)
    sums = jnp.where(before, sums, 0.0).astype(BF16)
    pick = (
        lax.broadcasted_iota(jnp.int32, (512, T), 0) // 128
        == lax.broadcasted_iota(jnp.int32, (512, T), 1)
    ).astype(BF16)
    ddecay = nn(sums, pick)
    pick64 = (
        lax.broadcasted_iota(jnp.int32, (256, T), 0) // 64
        == lax.broadcasted_iota(jnp.int32, (256, T), 1)
    ).astype(BF16)
    dstep = nn((dscaled * MIX[...]).astype(BF16), pick64)
    dstep = dstep + ddecay * -jnp.exp(vec_ref[1:2])
    L2[:, 128:256] = (dstep * SIG[...]).astype(BF16)

    loads[16].wait()
    lhs1 = L1[...]
    places = {}
    for j in FAR:
        for k in range(4):
            index = ((x + j) % NX) * NZ + (z + FAR[k]) % NZ
            places[j, k] = pl.ds(pl.multiple_of(index * 256, 256), 256)
            PM[j, k] = nt(lhs1, WM[places[j, k], :])
    loads[17].wait()
    loads[18].wait()
    for copy in mine:
        copy.wait_recv()
    swap.wait_recv()
    L2[:, 0:128] = (own_state + AR[...].astype(F32)).astype(BF16)
    lhs2 = L2[...]
    first_core = c == 0
    to_mate = {}
    for k in range(4):
        for j in FAR:
            part = PM[j, k] + nn(lhs2, WS[:, places[j, k]])
            lower, upper_half = part[:, 0:128], part[:, 128:256]
            Q[j, k] = jnp.where(first_core, lower, upper_half)
            PS[j, k] = jnp.where(first_core, upper_half, lower).astype(BF16)
            to_mate[j, k] = go(remote(PS.at[j, k], PR.at[j, k], mate))

    arrived = set()

    def chip_sum(j, k, h):
        if (j, k) not in arrived:
            arrived.add((j, k))
            to_mate[j, k].wait_recv()
        return Q[j, k, pieces[h]] + PR[j, k, pieces[h]].astype(F32)

    sends = {}
    zcopies = {}
    totals = {}
    sides = ((2, to_opposite), (1, to_right), (3, to_left))

    def send_x(h, k):
        for n, (j, target) in enumerate(sides):
            XS[n, k, pieces[h]] = chip_sum(j, k, h).astype(BF16)
            sends[n, h, k] = go(remote(XS.at[n, k, pieces[h]], XR.at[n, k, pieces[h]], target))

    def send_z(h, k):
        value = chip_sum(0, k, h)
        for n in (1, 2, 0):
            sends[n, h, k].wait_recv()
            value = value + XR[n, k, pieces[h]].astype(F32)
        if k < 3:
            ZS[k, pieces[h]] = value.astype(BF16)
            zcopies[h, k] = go(
                remote(
                    ZS.at[k, pieces[h]], ZR.at[k, pieces[h]],
                    dev(place(x, (z + FAR[k]) % NZ, c)),
                )
            )
        else:
            totals[h] = value

    for h in range(H):
        for k in range(4):
            send_x(h, k)
    for h in range(H):
        for k in range(4):
            send_z(h, k)
    for h in range(H):
        total = totals[h]
        for k in (1, 2, 0):
            zcopies[h, k].wait_recv()
            total = total + ZR[k, pieces[h]].astype(F32)
        out_ref[pieces[h], :] = total.astype(BF16)
        last = hand_off(out_ref, h)

        @pl.when(s > 0)
        def _():
            for copy in last:
                copy.start()

    for copies in first:
        for copy in copies:
            copy.wait_send()
    for copy in pending:
        copy.wait_send()


N_COPIES = H * (4 + 12 + 16 + 12 + 3) + 2 + 1 + 16


def body(
    weight_main, weight_state, weight_step, weight_out, conv_main, conv_state, step_bias,
    decay_log, skip_gain, norm_gain, saved_main, saved_state, saved_step, output_grad,
):
    group = lax.axis_index("tensor") // 4
    wm = weight_main[0].reshape(4096, 512)
    ws = jnp.transpose(weight_state[0], (1, 2, 0))
    main = saved_main[0].reshape(T, 512)
    state = lax.dynamic_slice_in_dim(saved_state[0], group * 128, 128, 2).reshape(T, 256)
    cs = lax.dynamic_slice_in_dim(conv_state[0], group * 128, 128, 2).reshape(4, 256)
    stepin = jnp.pad(saved_step[0].astype(F32).T, ((0, 0), (0, 124)))
    vec = jnp.pad(
        jnp.concatenate([step_bias, decay_log, skip_gain], axis=0), ((0, 5), (0, 124))
    )
    vmem = pl.BlockSpec(memory_space=pltpu.VMEM)
    hbm = pl.BlockSpec(memory_space=pl.ANY)
    block = (T, T)
    wide = (T, 256)
    result = pl.pallas_call(
        kernel,
        out_shape=jax.ShapeDtypeStruct((T, T), BF16),
        in_specs=[hbm] * 3 + [vmem] * 9,
        out_specs=vmem,
        scratch_shapes=[
            pltpu.VMEM((4096, 512), BF16),
            pltpu.VMEM((16, 256, 256), BF16),
            pltpu.VMEM((256, 4096), BF16),
            pltpu.VMEM((2, 4, 4) + block, BF16),
            pltpu.VMEM((4, 4) + block, F32),
            pltpu.VMEM((4, 4) + block, BF16),
            pltpu.VMEM((4, 4) + block, BF16),
            pltpu.VMEM((3, 4) + block, BF16),
            pltpu.VMEM((3, 4) + block, BF16),
            pltpu.VMEM((3,) + block, BF16),
            pltpu.VMEM((3,) + block, BF16),
            pltpu.VMEM(wide, F32),
            pltpu.VMEM(wide, F32),
            pltpu.VMEM(wide, F32),
            pltpu.VMEM(wide, F32),
            pltpu.VMEM(wide, F32),
            pltpu.VMEM(wide, F32),
            pltpu.VMEM(wide, F32),
            pltpu.VMEM((4,) + block, F32),
            pltpu.VMEM(block, F32),
            pltpu.VMEM((2, T, 256), BF16),
            pltpu.VMEM((4,) + block, BF16),
            pltpu.VMEM(wide, BF16),
            pltpu.VMEM(block, F32),
            pltpu.VMEM((8, 256), F32),
            pltpu.VMEM((T, 512), BF16),
            pltpu.VMEM((T, 256), BF16),
            pltpu.VMEM(block, BF16),
            pltpu.VMEM(block, BF16),
            pltpu.VMEM((4, 4, T, 256), F32),
            pltpu.SemaphoreType.DMA((20,)),
            pltpu.SemaphoreType.DMA((N_COPIES,)),
            pltpu.SemaphoreType.DMA((N_COPIES,)),
        ],
        compiler_params=pltpu.CompilerParams(
            collective_id=0, has_side_effects=True, vmem_limit_bytes=48 * 1024 * 1024
        ),
        name="relay",
    )(wm, ws, weight_out[0], weight_step[0], main, state, stepin, vec, conv_main[0], cs, norm_gain, output_grad)
    return result[None]


def solution(mesh):
    return jax.shard_map(
        body,
        mesh=mesh,
        in_specs=(
            P("pipe", None, None, "tensor"),
            P("pipe", None, None, "tensor"),
            P("pipe", "tensor", None),
            P("pipe", "tensor", None),
            P("pipe", None, "tensor"),
            P("pipe", None, None, None),
            P("pipe", "tensor"),
            P("pipe", "tensor"),
            P("pipe", "tensor"),
            P("pipe", "tensor"),
            P("pipe", "dp", None, "tensor"),
            P("pipe", "dp", None, None),
            P("pipe", "tensor", "dp"),
            P("dp", "tensor"),
        ),
        out_specs=P("pipe", "dp", "tensor"),
        check_vma=False,
    )
```

```python
import jax
import jax.numpy as jnp
from jax import lax
from jax.experimental import pallas as pl
from jax.experimental.pallas import tpu as pltpu
from jax.sharding import PartitionSpec as P

F32 = jnp.float32
BF16 = jnp.bfloat16
HIGHEST = lax.Precision.HIGHEST
EPSILON = 1e-05
MESH = pl.DeviceIdType.MESH
NX = 4
NZ = 4
T = 128
FAR = (2, 1, 3, 0)
H = 1
TH = T // H


def nn(a, b, precision=None):
    return lax.dot_general(
        a, b, (((1,), (0,)), ((), ())), preferred_element_type=F32, precision=precision
    )


def nt(a, b, precision=None):
    return lax.dot_general(
        a, b, (((1,), (1,)), ((), ())), preferred_element_type=F32, precision=precision
    )


def shift_down(v, n, rows):
    if n == 0:
        return v
    return jnp.where(rows >= n, pltpu.roll(v, n, 0), 0.0)


def shift_up(v, n, rows):
    if n == 0:
        return v
    return jnp.where(rows < T - n, pltpu.roll(v, T - n, 0), 0.0)


def conv(v, taps, rows):
    out = taps[3:4] * v
    for k in range(3):
        out = out + taps[k : k + 1] * shift_down(v, 3 - k, rows)
    return out


def conv_back(v, taps, rows):
    out = taps[3:4] * v
    for k in range(3):
        out = out + taps[k : k + 1] * shift_up(v, 3 - k, rows)
    return out


def kernel(
    wm_hbm, ws_hbm, wo_hbm,
    wt_ref, main_ref, state_ref, stepin_ref, vec_ref, cm_ref, cs_ref, gain_ref, og_ref,
    out_ref,
    WM, WO, WS, G, Q, PS, PR, XS, XR, ZS, ZR,
    NRM, SGI, YSP, MIX, STL, DSM, DSS, EM, SC, WTC, SCM, BC, SIG, SK, L1, L2,
    wsem, ssem, rsem,
):
    s = lax.axis_index("pipe")
    t = lax.axis_index("tensor")
    x = t // 8
    z = (t // 2) % 4
    c = t % 2
    d = lax.axis_index("dp")
    right_x = (x + 1) % NX
    left_x = (x + 3) % NX
    below = (s + 3) % 4
    above = (s + 1) % 4

    def place(px, pz, pc):
        return (px * NZ + pz) * 2 + pc

    def dev(tt, ss=None):
        if ss is None:
            return {"tensor": tt}
        return {"pipe": ss, "tensor": tt}

    count = [0]
    pending = []

    def remote(src, dst, target):
        i = count[0]
        count[0] += 1
        return pltpu.make_async_remote_copy(
            src_ref=src, dst_ref=dst, send_sem=ssem.at[i], recv_sem=rsem.at[i],
            device_id=target, device_id_type=MESH,
        )

    def go(copy):
        copy.start()
        pending.append(copy)
        return copy

    mate = dev(place(x, z, 1 - c))
    to_right = dev(place(right_x, z, c))
    to_left = dev(place(left_x, z, c))
    to_opposite = dev(place((x + 2) % NX, z, c))
    pair_z = z + 1 - 2 * (z % 2)
    inner = z % 2 != d
    to_inner = {"tensor": place(x, pair_z, c), "dp": 1 - d}
    to_outer = {"tensor": t, "dp": 1 - d}

    barrier = pltpu.get_barrier_semaphore()
    partners = [mate, to_right, to_left, to_opposite, to_inner, to_outer]
    for o in (1, 2, 3):
        partners.append(dev(place(x, (z + o) % NZ, c)))
    for o in range(4):
        partners.append(dev(place(x, (z + o) % NZ, c), below))
        partners.append(dev(place(x, (z + o) % NZ, c), above))
    for p in partners:
        pl.semaphore_signal(barrier, inc=1, device_id=p, device_id_type=MESH)

    loads = [
        pltpu.make_async_copy(wo_hbm.at[:, pl.ds(i * 256, 256)], WO.at[i], wsem.at[i])
        for i in range(16)
    ]
    loads.append(pltpu.make_async_copy(wm_hbm, WM, wsem.at[16]))
    m = t % 4
    cuts = [(half, pl.ds(part * 2048, 2048)) for half in range(2) for part in range(2)]

    def columns(member, half, lanes):
        return WS.at[pl.ds(pl.multiple_of(half * 128 + member * 32, 32), 32), lanes]

    def own_columns(half, lanes):
        return ws_hbm.at[half, :, lanes]

    loads += [
        pltpu.make_async_copy(own_columns(*cut), columns(m, *cut), wsem.at[17 + q])
        for q, cut in enumerate(cuts)
    ]
    for load in loads:
        load.start()

    pl.semaphore_wait(barrier, len(partners))

    pieces = [pl.ds(h * TH, TH) for h in range(H)]
    hand_ids = list(range(count[0], count[0] + 4 * H))
    count[0] += 4 * H

    def hand_off(block, h):
        copies = []
        for n, o in enumerate(FAR):
            i = hand_ids[4 * h + n]
            copies.append(
                pltpu.make_async_remote_copy(
                    src_ref=block.at[pieces[h]], dst_ref=G.at[c, 0, (4 - o) % 4, pieces[h]],
                    send_sem=ssem.at[i], recv_sem=rsem.at[i],
                    device_id=dev(place(x, (z + o) % NZ, c), below), device_id_type=MESH,
                )
            )
        return copies

    first = [hand_off(og_ref, h) for h in range(H)]

    @pl.when(s == 0)
    def _():
        for copies in first:
            for copy in copies:
                copy.start()

    mine = [go(remote(own_columns(*cut), columns(m, *cut), mate)) for cut in cuts]
    swaps = [remote(own_columns(*cut), columns(m, *cut), to_inner) for cut in cuts]
    other = (m + 2) % 4
    passes = [remote(columns(other, *cut), columns(other, *cut), to_outer) for cut in cuts]
    shares = [remote(columns(other, *cut), columns(other, *cut), mate) for cut in cuts]

    @pl.when(inner)
    def _():
        for copy in swaps:
            copy.start()

    def relay(chosen):
        for q in chosen:
            swaps[q].wait_recv()
            passes[q].start()
            shares[q].start()

    def accept():
        for q in range(4):
            passes[q].wait_recv()
            shares[q].start()

    early = s != 3
    WS[256:384, :] = jnp.zeros((128, 4096), BF16)
    WS[256:260, :] = wt_ref[...]

    rows = lax.broadcasted_iota(jnp.int32, (T, 256), 0)
    ri = lax.broadcasted_iota(jnp.int32, (T, T), 0)
    ci = lax.broadcasted_iota(jnp.int32, (T, T), 1)
    causal = ri >= ci
    rep = (
        lax.broadcasted_iota(jnp.int32, (T, 256), 0)
        == lax.broadcasted_iota(jnp.int32, (T, 256), 1) // 64
    ).astype(F32)
    gate = main_ref[:, 0:256].astype(F32)
    cm = cm_ref[...]
    cs = cs_ref[...]
    mixed = conv(main_ref[:, 256:512].astype(F32), cm, rows)
    sig = jax.nn.sigmoid(mixed)
    mix = mixed * sig
    DSM[...] = sig * (1.0 + mixed * (1.0 - sig))
    MIX[...] = mix
    states = conv(state_ref[...].astype(F32), cs, rows)
    sig = jax.nn.sigmoid(states)
    DSS[...] = sig * (1.0 + states * (1.0 - sig))
    states = states * sig
    BC[...] = states.astype(BF16)
    scores = nt(states[:, 128:256], states[:, 0:128], HIGHEST)
    SC[...] = scores
    vec = vec_ref[...]
    raw = stepin_ref[...] + vec[0:1]
    SIG[...] = jax.nn.sigmoid(raw)
    step = jnp.maximum(raw, 0.0) + jnp.log1p(jnp.exp(-jnp.abs(raw)))
    rate = -jnp.exp(vec[1:2])
    run_col = nn(causal.astype(F32), step * rate, HIGHEST)
    run_row = run_col.T
    stepl = nn(step, rep, HIGHEST)
    STL[...] = stepl
    SK[...] = nn(vec, rep, HIGHEST)
    skipl = SK[2:3]
    scaled = mix * stepl
    low = ci < 64
    ys = []
    for pair in range(2):
        sp = scaled[:, pair * 128 : pair * 128 + 128]
        acc = None
        for half in range(2):
            h = pair * 2 + half
            differ = run_col[:, h : h + 1] - run_row[h : h + 1, :]
            em = jnp.where(causal, jnp.exp(jnp.where(causal, differ, 0.0)), 0.0)
            EM[h] = em
            w = em * scores
            WTC[pair, :, half * 128 : half * 128 + 128] = w.T.astype(BF16)
            keep = low if half == 0 else jnp.logical_not(low)
            sh = jnp.where(keep, sp, 0.0)
            SCM[h] = sh.astype(BF16)
            part = nn(w, sh, HIGHEST)
            acc = part if acc is None else acc + part
        ys.append(acc)
    y = jnp.concatenate(ys, axis=1) + skipl * mix
    sg = jax.nn.sigmoid(gate)
    silu_gate = gate * sg
    gated = y * silu_gate
    inverse = lax.rsqrt(jnp.sum(gated * gated, axis=1, keepdims=True) * (1.0 / 256.0) + EPSILON)
    NRM[...] = gated * inverse
    SGI[...] = silu_gate * inverse
    YSP[...] = y * (sg * (1.0 + gate * (1.0 - sg))) * inverse

    ks = (0, 1, 3, 2)

    def spread(src_j, dst_j, target, h, k):
        return remote(G.at[c, src_j, k, pieces[h]], G.at[c, dst_j, k, pieces[h]], target)

    grid = [(h, k) for h in range(H) for k in ks]
    to_r = {hk: spread(0, 3, to_right, *hk) for hk in grid}
    to_l = {hk: spread(0, 1, to_left, *hk) for hk in grid}
    to_o = {hk: spread(0, 2, to_opposite, *hk) for hk in grid}
    to_m = {(j, h, k): spread(j, j, mate, h, k) for j in range(4) for h, k in grid}

    @pl.when(jnp.logical_and(early, inner))
    def _():
        relay(range(4))

    @pl.when(jnp.logical_and(early, jnp.logical_not(inner)))
    def _():
        accept()

    for h, k in grid:
        first[h][FAR.index((4 - k) % 4)].wait_recv()
        go(to_o[h, k])
        go(to_r[h, k])
        go(to_l[h, k])
        go(to_m[0, h, k])

    @pl.when(jnp.logical_and(s == 3, inner))
    def _():
        relay((0, 1))

    for h, k in grid:
        to_r[h, k].wait_recv()
        go(to_m[3, h, k])
        to_l[h, k].wait_recv()
        go(to_m[1, h, k])

    @pl.when(jnp.logical_and(s == 3, inner))
    def _():
        relay((2, 3))

    for i in range(16):
        loads[i].wait()
    totals = [None]

    def multiply(j):
        for k in ks:
            for h in range(H):
                to_m[j, h, k].wait_recv()
            index = ((x + j) % NX) * NZ + (z + k) % NZ
            block = jnp.concatenate([G[0, j, k], G[1, j, k]], axis=1)
            part = nt(block, WO[index])
            totals[0] = part if totals[0] is None else totals[0] + part

    multiply(0)
    multiply(3)
    for h, k in grid:
        to_o[h, k].wait_recv()
        go(to_m[2, h, k])
    multiply(1)
    multiply(2)
    acc = totals[0]

    dn = acc * gain_ref[...]
    nrm = NRM[...]
    mu = jnp.sum(dn * nrm, axis=1, keepdims=True) * (1.0 / 256.0)
    e = dn - nrm * mu
    dy = e * SGI[...]
    L1[:, 0:256] = (e * YSP[...]).astype(BF16)
    dyb = dy.astype(BF16)
    ds = None
    masks = []
    for h in range(4):
        a = nt(dyb[:, h // 2 * 128 : h // 2 * 128 + 128], SCM[h]) * EM[h]
        ds = a if ds is None else ds + a
        masks.append((a * SC[...]).astype(BF16))
    db = nn(ds.T.astype(BF16), BC[:, 128:256])
    dc = nn(ds.astype(BF16), BC[:, 0:128])
    dstate = jnp.concatenate([db, dc], axis=1) * DSS[...]
    L2[:, 0:256] = conv_back(dstate, cs_ref[...], rows).astype(BF16)
    dscs = []
    for pair in range(2):
        dyp = dyb[:, pair * 128 : pair * 128 + 128]
        zero = jnp.zeros_like(dyp)
        both = jnp.concatenate([jnp.where(low, dyp, zero), jnp.where(low, zero, dyp)], axis=0)
        dscs.append(nn(WTC[pair], both))
    dscaled = jnp.concatenate(dscs, axis=1)
    dmix = (dscaled * STL[...] + SK[2:3] * dy) * DSM[...]
    L1[:, 256:512] = conv_back(dmix, cm_ref[...], rows).astype(BF16)
    upper = (ci >= ri).astype(BF16)
    sums = nn(upper, jnp.concatenate(masks, axis=1))
    before = jnp.concatenate([ci < ri] * 4, axis=1)
    sums = jnp.where(before, sums, 0.0).astype(BF16)
    pick = (
        lax.broadcasted_iota(jnp.int32, (512, T), 0) // 128
        == lax.broadcasted_iota(jnp.int32, (512, T), 1)
    ).astype(BF16)
    ddecay = nn(sums, pick)
    pick64 = (
        lax.broadcasted_iota(jnp.int32, (256, T), 0) // 64
        == lax.broadcasted_iota(jnp.int32, (256, T), 1)
    ).astype(BF16)
    dstep = nn((dscaled * MIX[...]).astype(BF16), pick64)
    dstep = dstep + ddecay * -jnp.exp(vec_ref[1:2])
    L2[:, 256:384] = (dstep * SIG[...]).astype(BF16)

    @pl.when(jnp.logical_and(s == 3, jnp.logical_not(inner)))
    def _():
        accept()

    for load in loads[16:]:
        load.wait()
    for copy in mine + shares:
        copy.wait_recv()
    lhs1 = L1[...]
    lhs2 = L2[...]
    first_core = c == 0
    to_mate = {}

    def input_block(j, k):
        index = ((x + j) % NX) * NZ + (z + FAR[k]) % NZ
        at = pl.ds(pl.multiple_of(index * 256, 256), 256)
        part = nt(lhs1, WM[at, :]) + nn(lhs2, WS[:, at])
        lower, upper_half = part[:, 0:128], part[:, 128:256]
        Q[j, k] = jnp.where(first_core, lower, upper_half)
        PS[j, k] = jnp.where(first_core, upper_half, lower).astype(BF16)
        to_mate[j, k] = go(remote(PS.at[j, k], PR.at[j, k], mate))

    arrived = set()

    def chip_sum(j, k, h):
        if (j, k) not in arrived:
            arrived.add((j, k))
            to_mate[j, k].wait_recv()
        return Q[j, k, pieces[h]] + PR[j, k, pieces[h]].astype(F32)

    sends = {}
    zcopies = {}
    totals = {}
    sides = ((2, to_opposite), (1, to_right), (3, to_left))

    def send_x(h, k):
        for n, (j, target) in enumerate(sides):
            XS[n, k, pieces[h]] = chip_sum(j, k, h).astype(BF16)
            sends[n, h, k] = go(remote(XS.at[n, k, pieces[h]], XR.at[n, k, pieces[h]], target))

    def send_z(h, k):
        value = chip_sum(0, k, h)
        for n in (1, 2, 0):
            sends[n, h, k].wait_recv()
            value = value + XR[n, k, pieces[h]].astype(F32)
        if k < 3:
            ZS[k, pieces[h]] = value.astype(BF16)
            zcopies[h, k] = go(
                remote(
                    ZS.at[k, pieces[h]], ZR.at[k, pieces[h]],
                    dev(place(x, (z + FAR[k]) % NZ, c)),
                )
            )
        else:
            totals[h] = value

    for k in range(5):
        if k < 4:
            for j in FAR:
                input_block(j, k)
        if k > 0:
            for h in range(H):
                send_x(h, k - 1)
    for h in range(H):
        for k in range(4):
            send_z(h, k)
    for h in range(H):
        total = totals[h]
        for k in (1, 2, 0):
            zcopies[h, k].wait_recv()
            total = total + ZR[k, pieces[h]].astype(F32)
        out_ref[pieces[h], :] = total.astype(BF16)
        last = hand_off(out_ref, h)

        @pl.when(s > 0)
        def _():
            for copy in last:
                copy.start()

    for copies in first:
        for copy in copies:
            copy.wait_send()
    for copy in pending + shares:
        copy.wait_send()

    @pl.when(inner)
    def _():
        for copy in swaps + passes:
            copy.wait_send()


N_COPIES = H * (4 + 12 + 16 + 12 + 3) + 16 + 16


def body(
    weight_main, weight_state, weight_step, weight_out, conv_main, conv_state, step_bias,
    decay_log, skip_gain, norm_gain, saved_main, saved_state, saved_step, output_grad,
):
    group = lax.axis_index("tensor") // 4
    wm = weight_main[0].reshape(4096, 512)
    ws = jnp.transpose(weight_state[0], (1, 2, 0))
    main = saved_main[0].reshape(T, 512)
    state = lax.dynamic_slice_in_dim(saved_state[0], group * 128, 128, 2).reshape(T, 256)
    cs = lax.dynamic_slice_in_dim(conv_state[0], group * 128, 128, 2).reshape(4, 256)
    stepin = jnp.pad(saved_step[0].astype(F32).T, ((0, 0), (0, 124)))
    vec = jnp.pad(
        jnp.concatenate([step_bias, decay_log, skip_gain], axis=0), ((0, 5), (0, 124))
    )
    vmem = pl.BlockSpec(memory_space=pltpu.VMEM)
    hbm = pl.BlockSpec(memory_space=pl.ANY)
    block = (T, T)
    wide = (T, 256)
    result = pl.pallas_call(
        kernel,
        out_shape=jax.ShapeDtypeStruct((T, T), BF16),
        in_specs=[hbm] * 3 + [vmem] * 9,
        out_specs=vmem,
        scratch_shapes=[
            pltpu.VMEM((4096, 512), BF16),
            pltpu.VMEM((16, 256, 256), BF16),
            pltpu.VMEM((384, 4096), BF16),
            pltpu.VMEM((2, 4, 4) + block, BF16),
            pltpu.VMEM((4, 4) + block, F32),
            pltpu.VMEM((4, 4) + block, BF16),
            pltpu.VMEM((4, 4) + block, BF16),
            pltpu.VMEM((3, 4) + block, BF16),
            pltpu.VMEM((3, 4) + block, BF16),
            pltpu.VMEM((3,) + block, BF16),
            pltpu.VMEM((3,) + block, BF16),
            pltpu.VMEM(wide, F32),
            pltpu.VMEM(wide, F32),
            pltpu.VMEM(wide, F32),
            pltpu.VMEM(wide, F32),
            pltpu.VMEM(wide, F32),
            pltpu.VMEM(wide, F32),
            pltpu.VMEM(wide, F32),
            pltpu.VMEM((4,) + block, F32),
            pltpu.VMEM(block, F32),
            pltpu.VMEM((2, T, 256), BF16),
            pltpu.VMEM((4,) + block, BF16),
            pltpu.VMEM(wide, BF16),
            pltpu.VMEM(block, F32),
            pltpu.VMEM((8, 256), F32),
            pltpu.VMEM((T, 512), BF16),
            pltpu.VMEM((T, 384), BF16),
            pltpu.SemaphoreType.DMA((21,)),
            pltpu.SemaphoreType.DMA((N_COPIES,)),
            pltpu.SemaphoreType.DMA((N_COPIES,)),
        ],
        compiler_params=pltpu.CompilerParams(
            collective_id=0, has_side_effects=True, vmem_limit_bytes=48 * 1024 * 1024
        ),
        name="relay",
    )(wm, ws, weight_out[0], weight_step[0], main, state, stepin, vec, conv_main[0], cs, norm_gain, output_grad)
    return result[None]


def solution(mesh):
    return jax.shard_map(
        body,
        mesh=mesh,
        in_specs=(
            P("pipe", None, None, "tensor"),
            P("pipe", None, None, "tensor"),
            P("pipe", "tensor", None),
            P("pipe", "tensor", None),
            P("pipe", None, "tensor"),
            P("pipe", None, None, None),
            P("pipe", "tensor"),
            P("pipe", "tensor"),
            P("pipe", "tensor"),
            P("pipe", "tensor"),
            P("pipe", "dp", None, "tensor"),
            P("pipe", "dp", None, None),
            P("pipe", "tensor", "dp"),
            P("dp", "tensor"),
        ),
        out_specs=P("pipe", "dp", "tensor"),
        check_vma=False,
    )
```

```python
import jax
import jax.numpy as jnp
from jax import lax
from jax.experimental import pallas as pl
from jax.experimental.pallas import tpu as pltpu
from jax.sharding import PartitionSpec as P

F32 = jnp.float32
BF16 = jnp.bfloat16
HIGHEST = lax.Precision.HIGHEST
EPSILON = 1e-05
MESH = pl.DeviceIdType.MESH
NX = 4
NZ = 4
T = 128
FAR = (2, 1, 3, 0)
H = 1
TH = T // H


def nn(a, b, precision=None):
    return lax.dot_general(
        a, b, (((1,), (0,)), ((), ())), preferred_element_type=F32, precision=precision
    )


def nt(a, b, precision=None):
    return lax.dot_general(
        a, b, (((1,), (1,)), ((), ())), preferred_element_type=F32, precision=precision
    )


def shift_down(v, n, rows):
    if n == 0:
        return v
    return jnp.where(rows >= n, pltpu.roll(v, n, 0), 0.0)


def shift_up(v, n, rows):
    if n == 0:
        return v
    return jnp.where(rows < T - n, pltpu.roll(v, T - n, 0), 0.0)


def conv(v, taps, rows):
    out = taps[3:4] * v
    for k in range(3):
        out = out + taps[k : k + 1] * shift_down(v, 3 - k, rows)
    return out


def conv_back(v, taps, rows):
    out = taps[3:4] * v
    for k in range(3):
        out = out + taps[k : k + 1] * shift_up(v, 3 - k, rows)
    return out


def kernel(
    wm_hbm, ws_hbm, wo_hbm,
    bias_hbm, decay_hbm, skip_hbm,
    wt_hbm, main_hbm, state_hbm, stepin_hbm, cm_hbm, cs_hbm, gain_hbm, og_hbm,
    out_ref,
    bias_ref, decay_ref, skip_ref, wt_ref, main_ref, state_ref, stepin_ref, cm_ref, cs_ref, gain_ref,
    RAW, W, WO, STEP, G, Q, PS, PR, XS, XR, ZS, ZR,
    NRM, SGI, YSP, MIX, STL, DSM, DSS, EM, SC, WTC, SCM, BC, SIG, SK, CS, L,
    wsem, ssem, rsem,
):
    s = lax.axis_index("pipe")
    t = lax.axis_index("tensor")
    x = t // 8
    z = (t // 2) % 4
    c = t % 2
    d = lax.axis_index("dp")
    right_x = (x + 1) % NX
    left_x = (x + 3) % NX
    below = (s + 3) % 4
    above = (s + 1) % 4

    def place(px, pz, pc):
        return (px * NZ + pz) * 2 + pc

    def dev(tt, ss=None):
        if ss is None:
            return {"tensor": tt}
        return {"pipe": ss, "tensor": tt}

    count = [0]
    pending = []

    def remote(src, dst, target):
        i = count[0]
        count[0] += 1
        return pltpu.make_async_remote_copy(
            src_ref=src, dst_ref=dst, send_sem=ssem.at[i], recv_sem=rsem.at[i],
            device_id=target, device_id_type=MESH,
        )

    def go(copy):
        copy.start()
        pending.append(copy)
        return copy

    mate = dev(place(x, z, 1 - c))
    to_right = dev(place(right_x, z, c))
    to_left = dev(place(left_x, z, c))
    to_opposite = dev(place((x + 2) % NX, z, c))
    pair_z = z + 1 - 2 * (z % 2)
    inner = z % 2 != d
    to_inner = {"tensor": place(x, pair_z, c), "dp": 1 - d}
    to_outer = {"tensor": t, "dp": 1 - d}

    barrier = pltpu.get_barrier_semaphore()
    partners = [mate, to_right, to_left, to_opposite, to_inner, to_outer]
    for o in (1, 2, 3):
        partners.append(dev(place(x, (z + o) % NZ, c)))
    for o in range(4):
        partners.append(dev(place(x, (z + o) % NZ, c), below))
        partners.append(dev(place(x, (z + o) % NZ, c), above))
    for p in partners:
        pl.semaphore_signal(barrier, inc=1, device_id=p, device_id_type=MESH)

    group = pl.ds(pl.multiple_of(t // 4 * 128, 128), 128)
    small = [
        (main_hbm, main_ref), (state_hbm.at[:, :, group], state_ref), (cm_hbm, cm_ref),
        (cs_hbm.at[:, :, group], cs_ref), (stepin_hbm, stepin_ref), (bias_hbm, bias_ref),
        (decay_hbm, decay_ref), (skip_hbm, skip_ref), (gain_hbm, gain_ref), (wt_hbm, wt_ref),
    ]
    small = [pltpu.make_async_copy(src, dst, wsem.at[21 + i]) for i, (src, dst) in enumerate(small)]
    for load in small:
        load.start()
    loads = [
        pltpu.make_async_copy(wo_hbm.at[:, pl.ds(i * 256, 256)], WO.at[i], wsem.at[i])
        for i in range(16)
    ]
    loads.append(pltpu.make_async_copy(wm_hbm, RAW, wsem.at[16]))
    m = t % 4
    cuts = [(half, pl.ds(part * 2048, 2048)) for half in range(2) for part in range(2)]

    def columns(member, half, lanes):
        return W.at[pl.ds(pl.multiple_of(512 + half * 128 + member * 32, 32), 32), lanes]

    def own_columns(half, lanes):
        return ws_hbm.at[half, :, lanes]

    loads += [
        pltpu.make_async_copy(own_columns(*cut), columns(m, *cut), wsem.at[17 + q])
        for q, cut in enumerate(cuts)
    ]
    for load in loads:
        load.start()

    pl.semaphore_wait(barrier, len(partners))

    pieces = [pl.ds(h * TH, TH) for h in range(H)]
    hand_ids = list(range(count[0], count[0] + 4 * H))
    count[0] += 4 * H

    def hand_off(block, h):
        copies = []
        for n, o in enumerate(FAR):
            i = hand_ids[4 * h + n]
            copies.append(
                pltpu.make_async_remote_copy(
                    src_ref=block.at[pieces[h]], dst_ref=G.at[c, 0, (4 - o) % 4, pieces[h]],
                    send_sem=ssem.at[i], recv_sem=rsem.at[i],
                    device_id=dev(place(x, (z + o) % NZ, c), below), device_id_type=MESH,
                )
            )
        return copies

    first = [hand_off(og_hbm, h) for h in range(H)]

    @pl.when(s == 0)
    def _():
        for copies in first:
            for copy in copies:
                copy.start()

    mine = [go(remote(own_columns(*cut), columns(m, *cut), mate)) for cut in cuts]
    swaps = [remote(own_columns(*cut), columns(m, *cut), to_inner) for cut in cuts]
    other = (m + 2) % 4
    passes = [remote(columns(other, *cut), columns(other, *cut), to_outer) for cut in cuts]
    shares = [remote(columns(other, *cut), columns(other, *cut), mate) for cut in cuts]

    @pl.when(inner)
    def _():
        for copy in swaps:
            copy.start()

    def relay(chosen):
        for q in chosen:
            swaps[q].wait_recv()
            passes[q].start()
            shares[q].start()

    def accept():
        for q in range(4):
            passes[q].wait_recv()
            shares[q].start()

    early = s != 3
    for load in small:
        load.wait()
    W[768:896, :] = jnp.zeros((128, 4096), BF16)
    W[768:772, :] = wt_ref[...]

    apart_row = lax.broadcasted_iota(jnp.int32, (256, 256), 0)
    apart_col = lax.broadcasted_iota(jnp.int32, (256, 256), 1)
    apart = (apart_col == 2 * (apart_row % 128) + apart_row // 128).astype(BF16)

    def turn(first_block, last_block):
        def one(i, carry):
            at = pl.ds(pl.multiple_of(i * 128, 128), 128)
            both = lax.dot_general(
                RAW[at].reshape(256, 256), apart, (((0,), (1,)), ((), ())),
                preferred_element_type=F32,
            ).astype(BF16)
            W[0:256, at] = both[:, 0:128]
            W[256:512, at] = both[:, 128:256]
            return carry

        lax.fori_loop(first_block, last_block, one, 0, unroll=4)

    rows = lax.broadcasted_iota(jnp.int32, (T, 256), 0)
    ri = lax.broadcasted_iota(jnp.int32, (T, T), 0)
    ci = lax.broadcasted_iota(jnp.int32, (T, T), 1)
    causal = ri >= ci
    rep = (
        lax.broadcasted_iota(jnp.int32, (T, 256), 0)
        == lax.broadcasted_iota(jnp.int32, (T, 256), 1) // 64
    ).astype(F32)
    pair_in = nn(apart, main_ref[...].reshape(256, 256))
    gate = pair_in[0:128]
    cm = cm_ref[...]
    cs = jnp.concatenate([cs_ref[:, 0, :], cs_ref[:, 1, :]], axis=1)
    CS[...] = cs
    mixed = conv(pair_in[128:256], cm, rows)
    sig = jax.nn.sigmoid(mixed)
    mix = mixed * sig
    DSM[...] = sig * (1.0 + mixed * (1.0 - sig))
    MIX[...] = mix
    pair_in = nn(apart, state_ref[...].reshape(256, 128))
    states = conv(jnp.concatenate([pair_in[0:128], pair_in[128:256]], axis=1), cs, rows)
    sig = jax.nn.sigmoid(states)
    DSS[...] = sig * (1.0 + states * (1.0 - sig))
    states = states * sig
    BC[...] = states.astype(BF16)
    scores = nt(states[:, 128:256], states[:, 0:128], HIGHEST)
    SC[...] = scores
    heads = lax.broadcasted_iota(jnp.int32, (1, T), 1)
    channels = lax.broadcasted_iota(jnp.int32, (1, 256), 1) // 64

    def by_lane(ref, lanes):
        out = jnp.zeros(lanes.shape, F32)
        for h in range(4):
            out = jnp.where(lanes == h, ref[0, h], out)
        return out

    STEP[...] = jnp.zeros((T, T), F32)
    STEP[0:4, :] = stepin_ref[...].astype(F32)
    raw = STEP[...].T + by_lane(bias_ref, heads)
    SIG[...] = jax.nn.sigmoid(raw)
    step = jnp.maximum(raw, 0.0) + jnp.log1p(jnp.exp(-jnp.abs(raw)))
    rate = -jnp.exp(by_lane(decay_ref, heads))
    SK[0:1, 0:128] = rate
    run_col = nn(causal.astype(F32), step * rate, HIGHEST)
    run_row = run_col.T
    stepl = nn(step, rep, HIGHEST)
    STL[...] = stepl
    skipl = by_lane(skip_ref, channels)
    SK[1:2] = skipl
    scaled = mix * stepl
    low = ci < 64
    ys = []
    for pair in range(2):
        sp = scaled[:, pair * 128 : pair * 128 + 128]
        acc = None
        for half in range(2):
            h = pair * 2 + half
            differ = run_col[:, h : h + 1] - run_row[h : h + 1, :]
            em = jnp.where(causal, jnp.exp(jnp.where(causal, differ, 0.0)), 0.0)
            EM[h] = em
            w = em * scores
            WTC[pair, :, half * 128 : half * 128 + 128] = w.T.astype(BF16)
            keep = low if half == 0 else jnp.logical_not(low)
            sh = jnp.where(keep, sp, 0.0)
            SCM[h] = sh.astype(BF16)
            part = nn(w, sh, HIGHEST)
            acc = part if acc is None else acc + part
        ys.append(acc)
    y = jnp.concatenate(ys, axis=1) + skipl * mix
    sg = jax.nn.sigmoid(gate)
    silu_gate = gate * sg
    gated = y * silu_gate
    inverse = lax.rsqrt(jnp.sum(gated * gated, axis=1, keepdims=True) * (1.0 / 256.0) + EPSILON)
    NRM[...] = gated * inverse
    SGI[...] = silu_gate * inverse
    YSP[...] = y * (sg * (1.0 + gate * (1.0 - sg))) * inverse

    ks = (0, 1, 3, 2)

    def spread(src_j, dst_j, target, h, k):
        return remote(G.at[c, src_j, k, pieces[h]], G.at[c, dst_j, k, pieces[h]], target)

    grid = [(h, k) for h in range(H) for k in ks]
    to_r = {hk: spread(0, 3, to_right, *hk) for hk in grid}
    to_l = {hk: spread(0, 1, to_left, *hk) for hk in grid}
    to_o = {hk: spread(0, 2, to_opposite, *hk) for hk in grid}
    to_m = {(j, h, k): spread(j, j, mate, h, k) for j in range(4) for h, k in grid}

    loads[16].wait()

    @pl.when(early)
    def _():
        turn(0, 32)

    @pl.when(jnp.logical_and(early, inner))
    def _():
        relay(range(4))

    @pl.when(jnp.logical_and(early, jnp.logical_not(inner)))
    def _():
        accept()

    for h, k in grid:
        first[h][FAR.index((4 - k) % 4)].wait_recv()
        go(to_o[h, k])
        go(to_r[h, k])
        go(to_l[h, k])
        go(to_m[0, h, k])

    @pl.when(jnp.logical_and(s == 3, inner))
    def _():
        relay((0, 1))

    @pl.when(s == 3)
    def _():
        turn(0, 24)

    for n, (h, k) in enumerate(grid):
        to_r[h, k].wait_recv()
        go(to_m[3, h, k])
        to_l[h, k].wait_recv()
        go(to_m[1, h, k])
        if n == 2 * H - 1:

            @pl.when(jnp.logical_and(s == 3, inner))
            def _():
                relay((2,))


    @pl.when(jnp.logical_and(s == 3, inner))
    def _():
        relay((3,))

    @pl.when(s == 3)
    def _():
        turn(24, 32)

    for i in range(16):
        loads[i].wait()
    totals = [None]

    def multiply(j):
        for k in ks:
            for h in range(H):
                to_m[j, h, k].wait_recv()
            index = ((x + j) % NX) * NZ + (z + k) % NZ
            block = jnp.concatenate([G[0, j, k], G[1, j, k]], axis=1)
            part = nt(block, WO[index])
            totals[0] = part if totals[0] is None else totals[0] + part

    multiply(0)
    multiply(3)
    for h, k in grid:
        to_o[h, k].wait_recv()
        go(to_m[2, h, k])
    multiply(1)
    multiply(2)
    acc = totals[0]

    dn = acc * gain_ref[...]
    nrm = NRM[...]
    mu = jnp.sum(dn * nrm, axis=1, keepdims=True) * (1.0 / 256.0)
    e = dn - nrm * mu
    dy = e * SGI[...]
    L[:, 0:256] = (e * YSP[...]).astype(BF16)
    dyb = dy.astype(BF16)
    ds = None
    masks = []
    for h in range(4):
        a = nt(dyb[:, h // 2 * 128 : h // 2 * 128 + 128], SCM[h]) * EM[h]
        ds = a if ds is None else ds + a
        masks.append((a * SC[...]).astype(BF16))
    db = nn(ds.T.astype(BF16), BC[:, 128:256])
    dc = nn(ds.astype(BF16), BC[:, 0:128])
    dstate = jnp.concatenate([db, dc], axis=1) * DSS[...]
    L[:, 512:768] = conv_back(dstate, CS[...], rows).astype(BF16)
    dscs = []
    for pair in range(2):
        dyp = dyb[:, pair * 128 : pair * 128 + 128]
        zero = jnp.zeros_like(dyp)
        both = jnp.concatenate([jnp.where(low, dyp, zero), jnp.where(low, zero, dyp)], axis=0)
        dscs.append(nn(WTC[pair], both))
    dscaled = jnp.concatenate(dscs, axis=1)
    dmix = (dscaled * STL[...] + SK[1:2] * dy) * DSM[...]
    L[:, 256:512] = conv_back(dmix, cm_ref[...], rows).astype(BF16)
    upper = (ci >= ri).astype(BF16)
    sums = nn(upper, jnp.concatenate(masks, axis=1))
    before = jnp.concatenate([ci < ri] * 4, axis=1)
    sums = jnp.where(before, sums, 0.0).astype(BF16)
    pick = (
        lax.broadcasted_iota(jnp.int32, (512, T), 0) // 128
        == lax.broadcasted_iota(jnp.int32, (512, T), 1)
    ).astype(BF16)
    ddecay = nn(sums, pick)
    pick64 = (
        lax.broadcasted_iota(jnp.int32, (256, T), 0) // 64
        == lax.broadcasted_iota(jnp.int32, (256, T), 1)
    ).astype(BF16)
    dstep = nn((dscaled * MIX[...]).astype(BF16), pick64)
    dstep = dstep + ddecay * SK[0:1, 0:128]
    L[:, 768:896] = (dstep * SIG[...]).astype(BF16)

    @pl.when(jnp.logical_and(s == 3, jnp.logical_not(inner)))
    def _():
        accept()

    for load in loads[17:]:
        load.wait()
    for copy in mine + shares:
        copy.wait_recv()
    lhs = L[...]
    first_core = c == 0
    to_mate = {}

    def input_block(j, k):
        index = ((x + j) % NX) * NZ + (z + FAR[k]) % NZ
        at = pl.ds(pl.multiple_of(index * 256, 256), 256)
        part = nn(lhs, W[:, at])
        lower, upper_half = part[:, 0:128], part[:, 128:256]
        Q[j, k] = jnp.where(first_core, lower, upper_half)
        PS[j, k] = jnp.where(first_core, upper_half, lower).astype(BF16)
        to_mate[j, k] = go(remote(PS.at[j, k], PR.at[j, k], mate))

    arrived = set()

    def chip_sum(j, k, h):
        if (j, k) not in arrived:
            arrived.add((j, k))
            to_mate[j, k].wait_recv()
        return Q[j, k, pieces[h]] + PR[j, k, pieces[h]].astype(F32)

    sends = {}
    zcopies = {}
    totals = {}
    sides = ((2, to_opposite), (1, to_right), (3, to_left))

    def send_x(h, k):
        for n, (j, target) in enumerate(sides):
            XS[n, k, pieces[h]] = chip_sum(j, k, h).astype(BF16)
            sends[n, h, k] = go(remote(XS.at[n, k, pieces[h]], XR.at[n, k, pieces[h]], target))

    def send_z(h, k):
        value = chip_sum(0, k, h)
        for n in (1, 2, 0):
            sends[n, h, k].wait_recv()
            value = value + XR[n, k, pieces[h]].astype(F32)
        if k < 3:
            ZS[k, pieces[h]] = value.astype(BF16)
            zcopies[h, k] = go(
                remote(
                    ZS.at[k, pieces[h]], ZR.at[k, pieces[h]],
                    dev(place(x, (z + FAR[k]) % NZ, c)),
                )
            )
        else:
            totals[h] = value

    for k in range(5):
        if k < 4:
            for j in FAR:
                input_block(j, k)
        if k > 0:
            for h in range(H):
                send_x(h, k - 1)
    for h in range(H):
        for k in range(4):
            send_z(h, k)
    for h in range(H):
        total = totals[h]
        for k in (1, 2, 0):
            zcopies[h, k].wait_recv()
            total = total + ZR[k, pieces[h]].astype(F32)
        out_ref[pieces[h], :] = total.astype(BF16)
        last = hand_off(out_ref, h)

        @pl.when(s > 0)
        def _():
            for copy in last:
                copy.start()

    for copies in first:
        for copy in copies:
            copy.wait_send()
    for copy in pending + shares:
        copy.wait_send()

    @pl.when(inner)
    def _():
        for copy in swaps + passes:
            copy.wait_send()


N_COPIES = H * (4 + 12 + 16 + 12 + 3) + 16 + 16


def body(
    weight_main, weight_state, weight_step, weight_out, conv_main, conv_state, step_bias,
    decay_log, skip_gain, norm_gain, saved_main, saved_state, saved_step, output_grad,
):
    ws = jnp.transpose(weight_state[0], (1, 2, 0))
    vmem = pl.BlockSpec(memory_space=pltpu.VMEM)
    hbm = pl.BlockSpec(memory_space=pltpu.HBM)
    block = (T, T)
    wide = (T, 256)
    result = pl.pallas_call(
        kernel,
        out_shape=jax.ShapeDtypeStruct((T, T), BF16),
        in_specs=[hbm] * 14,
        out_specs=vmem,
        scratch_shapes=[
            pltpu.SMEM((1, 4), F32),
            pltpu.SMEM((1, 4), F32),
            pltpu.SMEM((1, 4), F32),
            pltpu.VMEM((4, 4096), BF16),
            pltpu.VMEM((T, 2, 256), BF16),
            pltpu.VMEM((T, 2, 128), BF16),
            pltpu.VMEM((4, T), BF16),
            pltpu.VMEM((4, 256), F32),
            pltpu.VMEM((4, 2, 128), F32),
            pltpu.VMEM((1, 256), F32),
            pltpu.VMEM((4096, 2, 256), BF16),
            pltpu.VMEM((896, 4096), BF16),
            pltpu.VMEM((16, 256, 256), BF16),
            pltpu.VMEM(block, F32),
            pltpu.VMEM((2, 4, 4) + block, BF16),
            pltpu.VMEM((4, 4) + block, F32),
            pltpu.VMEM((4, 4) + block, BF16),
            pltpu.VMEM((4, 4) + block, BF16),
            pltpu.VMEM((3, 4) + block, BF16),
            pltpu.VMEM((3, 4) + block, BF16),
            pltpu.VMEM((3,) + block, BF16),
            pltpu.VMEM((3,) + block, BF16),
            pltpu.VMEM(wide, F32),
            pltpu.VMEM(wide, F32),
            pltpu.VMEM(wide, F32),
            pltpu.VMEM(wide, F32),
            pltpu.VMEM(wide, F32),
            pltpu.VMEM(wide, F32),
            pltpu.VMEM(wide, F32),
            pltpu.VMEM((4,) + block, F32),
            pltpu.VMEM(block, F32),
            pltpu.VMEM((2, T, 256), BF16),
            pltpu.VMEM((4,) + block, BF16),
            pltpu.VMEM(wide, BF16),
            pltpu.VMEM(block, F32),
            pltpu.VMEM((8, 256), F32),
            pltpu.VMEM((4, 256), F32),
            pltpu.VMEM((T, 896), BF16),
            pltpu.SemaphoreType.DMA((31,)),
            pltpu.SemaphoreType.DMA((N_COPIES,)),
            pltpu.SemaphoreType.DMA((N_COPIES,)),
        ],
        compiler_params=pltpu.CompilerParams(
            collective_id=0, has_side_effects=True, vmem_limit_bytes=67043328
        ),
        name="relay",
    )(
        weight_main[0], ws, weight_out[0], step_bias, decay_log, skip_gain, weight_step[0],
        saved_main[0], saved_state[0], saved_step[0], conv_main[0], conv_state[0], norm_gain,
        output_grad,
    )
    return result[None]


def solution(mesh):
    return jax.shard_map(
        body,
        mesh=mesh,
        in_specs=(
            P("pipe", None, None, "tensor"),
            P("pipe", None, None, "tensor"),
            P("pipe", "tensor", None),
            P("pipe", "tensor", None),
            P("pipe", None, "tensor"),
            P("pipe", None, None, None),
            P("pipe", "tensor"),
            P("pipe", "tensor"),
            P("pipe", "tensor"),
            P("pipe", "tensor"),
            P("pipe", "dp", None, "tensor"),
            P("pipe", "dp", None, None),
            P("pipe", "tensor", "dp"),
            P("dp", "tensor"),
        ),
        out_specs=P("pipe", "dp", "tensor"),
        check_vma=False,
    )
```

```python
import jax
import jax.numpy as jnp
from jax import lax
from jax.experimental import pallas as pl
from jax.experimental.pallas import tpu as pltpu
from jax.sharding import PartitionSpec as P

F32 = jnp.float32
BF16 = jnp.bfloat16
HIGHEST = lax.Precision.HIGHEST
EPSILON = 1e-05
MESH = pl.DeviceIdType.MESH
NX = 4
NZ = 4
T = 128
FAR = (2, 1, 3, 0)
H = 1
TH = T // H


def nn(a, b, precision=None):
    return lax.dot_general(
        a, b, (((1,), (0,)), ((), ())), preferred_element_type=F32, precision=precision
    )


def nt(a, b, precision=None):
    return lax.dot_general(
        a, b, (((1,), (1,)), ((), ())), preferred_element_type=F32, precision=precision
    )


def shift_down(v, n, rows):
    if n == 0:
        return v
    return jnp.where(rows >= n, pltpu.roll(v, n, 0), 0.0)


def shift_up(v, n, rows):
    if n == 0:
        return v
    return jnp.where(rows < T - n, pltpu.roll(v, T - n, 0), 0.0)


def conv(v, taps, rows):
    out = taps[3:4] * v
    for k in range(3):
        out = out + taps[k : k + 1] * shift_down(v, 3 - k, rows)
    return out


def conv_back(v, taps, rows):
    out = taps[3:4] * v
    for k in range(3):
        out = out + taps[k : k + 1] * shift_up(v, 3 - k, rows)
    return out


def kernel(
    wm_hbm, ws_hbm, wo_hbm,
    bias_hbm, decay_hbm, skip_hbm,
    wt_hbm, main_hbm, state_hbm, stepin_hbm, cm_hbm, cs_hbm, gain_hbm, og_hbm,
    out_ref,
    bias_ref, decay_ref, skip_ref, wt_ref, main_ref, state_ref, stepin_ref, cm_ref, cs_ref, gain_ref,
    RAW, W, WO, STEP, G, Q, PS, PR, XS, XR, ZS, ZR,
    NRM, SGI, YSP, MIX, STL, DSM, DSS, EM, SC, WTC, SCM, BC, SIG, SK, CS, L, ACC,
    wsem, ssem, rsem,
):
    s = lax.axis_index("pipe")
    t = lax.axis_index("tensor")
    x = t // 8
    z = (t // 2) % 4
    c = t % 2
    d = lax.axis_index("dp")
    right_x = (x + 1) % NX
    left_x = (x + 3) % NX
    below = (s + 3) % 4
    above = (s + 1) % 4

    def place(px, pz, pc):
        return (px * NZ + pz) * 2 + pc

    def dev(tt, ss=None):
        if ss is None:
            return {"tensor": tt}
        return {"pipe": ss, "tensor": tt}

    count = [0]
    pending = []

    def remote(src, dst, target):
        i = count[0]
        count[0] += 1
        return pltpu.make_async_remote_copy(
            src_ref=src, dst_ref=dst, send_sem=ssem.at[i], recv_sem=rsem.at[i],
            device_id=target, device_id_type=MESH,
        )

    def go(copy):
        copy.start()
        pending.append(copy)
        return copy

    mate = dev(place(x, z, 1 - c))
    to_right = dev(place(right_x, z, c))
    to_left = dev(place(left_x, z, c))
    to_opposite = dev(place((x + 2) % NX, z, c))
    pair_z = z + 1 - 2 * (z % 2)
    inner = z % 2 != d
    to_inner = {"tensor": place(x, pair_z, c), "dp": 1 - d}
    to_outer = {"tensor": t, "dp": 1 - d}

    barrier = pltpu.get_barrier_semaphore()
    partners = [mate, to_right, to_left, to_opposite, to_inner, to_outer]
    for o in (1, 2, 3):
        partners.append(dev(place(x, (z + o) % NZ, c)))
    for o in range(4):
        partners.append(dev(place(x, (z + o) % NZ, c), below))
        partners.append(dev(place(x, (z + o) % NZ, c), above))
    for p in partners:
        pl.semaphore_signal(barrier, inc=1, device_id=p, device_id_type=MESH)

    group = pl.ds(pl.multiple_of(t // 4 * 128, 128), 128)
    small = [
        (main_hbm, main_ref), (state_hbm.at[:, :, group], state_ref), (cm_hbm, cm_ref),
        (cs_hbm.at[:, :, group], cs_ref), (stepin_hbm, stepin_ref), (bias_hbm, bias_ref),
        (decay_hbm, decay_ref), (skip_hbm, skip_ref), (gain_hbm, gain_ref), (wt_hbm, wt_ref),
    ]
    small = [pltpu.make_async_copy(src, dst, wsem.at[21 + i]) for i, (src, dst) in enumerate(small)]
    for load in small:
        load.start()
    loads = [
        pltpu.make_async_copy(wo_hbm.at[:, pl.ds(i * 256, 256)], WO.at[i], wsem.at[i])
        for i in range(16)
    ]
    loads.append(pltpu.make_async_copy(wm_hbm, RAW, wsem.at[16]))
    m = t % 4
    cuts = [(half, pl.ds(part * 2048, 2048)) for half in range(2) for part in range(2)]

    def columns(member, half, lanes):
        return W.at[pl.ds(pl.multiple_of(512 + half * 128 + member * 32, 32), 32), lanes]

    def own_columns(half, lanes):
        return ws_hbm.at[half, :, lanes]

    loads += [
        pltpu.make_async_copy(own_columns(*cut), columns(m, *cut), wsem.at[17 + q])
        for q, cut in enumerate(cuts)
    ]
    for load in loads:
        load.start()

    pl.semaphore_wait(barrier, len(partners))

    pieces = [pl.ds(h * TH, TH) for h in range(H)]
    hand_ids = list(range(count[0], count[0] + 4 * H))
    count[0] += 4 * H

    def hand_off(block, h):
        copies = []
        for n, o in enumerate(FAR):
            i = hand_ids[4 * h + n]
            copies.append(
                pltpu.make_async_remote_copy(
                    src_ref=block.at[pieces[h]], dst_ref=G.at[c, (4 - o) % 4, 0, pieces[h]],
                    send_sem=ssem.at[i], recv_sem=rsem.at[i],
                    device_id=dev(place(x, (z + o) % NZ, c), below), device_id_type=MESH,
                )
            )
        return copies

    first = [hand_off(og_hbm, h) for h in range(H)]

    @pl.when(s == 0)
    def _():
        for copies in first:
            for copy in copies:
                copy.start()

    mine = [go(remote(own_columns(*cut), columns(m, *cut), mate)) for cut in cuts]
    swaps = [remote(own_columns(*cut), columns(m, *cut), to_inner) for cut in cuts]
    other = (m + 2) % 4
    passes = [remote(columns(other, *cut), columns(other, *cut), to_outer) for cut in cuts]
    shares = [remote(columns(other, *cut), columns(other, *cut), mate) for cut in cuts]

    @pl.when(inner)
    def _():
        for copy in swaps:
            copy.start()

    def relay(chosen):
        for q in chosen:
            swaps[q].wait_recv()
            passes[q].start()
            shares[q].start()

    def accept():
        for q in range(4):
            passes[q].wait_recv()
            shares[q].start()

    early = s != 3
    for load in small:
        load.wait()
    W[768:896, :] = jnp.zeros((128, 4096), BF16)
    W[768:772, :] = wt_ref[...]

    apart_row = lax.broadcasted_iota(jnp.int32, (256, 256), 0)
    apart_col = lax.broadcasted_iota(jnp.int32, (256, 256), 1)
    apart = (apart_col == 2 * (apart_row % 128) + apart_row // 128).astype(BF16)

    def turn(first_block, last_block):
        def one(i, carry):
            at = pl.ds(pl.multiple_of(i * 128, 128), 128)
            both = lax.dot_general(
                RAW[at].reshape(256, 256), apart, (((0,), (1,)), ((), ())),
                preferred_element_type=F32,
            ).astype(BF16)
            W[0:256, at] = both[:, 0:128]
            W[256:512, at] = both[:, 128:256]
            return carry

        lax.fori_loop(first_block, last_block, one, 0, unroll=4)

    rows = lax.broadcasted_iota(jnp.int32, (T, 256), 0)
    ri = lax.broadcasted_iota(jnp.int32, (T, T), 0)
    ci = lax.broadcasted_iota(jnp.int32, (T, T), 1)
    causal = ri >= ci
    rep = (
        lax.broadcasted_iota(jnp.int32, (T, 256), 0)
        == lax.broadcasted_iota(jnp.int32, (T, 256), 1) // 64
    ).astype(F32)
    pair_in = nn(apart, main_ref[...].reshape(256, 256))
    gate = pair_in[0:128]
    cm = cm_ref[...]
    cs = jnp.concatenate([cs_ref[:, 0, :], cs_ref[:, 1, :]], axis=1)
    CS[...] = cs
    mixed = conv(pair_in[128:256], cm, rows)
    sig = jax.nn.sigmoid(mixed)
    mix = mixed * sig
    DSM[...] = sig * (1.0 + mixed * (1.0 - sig))
    MIX[...] = mix
    pair_in = nn(apart, state_ref[...].reshape(256, 128))
    states = conv(jnp.concatenate([pair_in[0:128], pair_in[128:256]], axis=1), cs, rows)
    sig = jax.nn.sigmoid(states)
    DSS[...] = sig * (1.0 + states * (1.0 - sig))
    states = states * sig
    BC[...] = states.astype(BF16)
    scores = nt(states[:, 128:256], states[:, 0:128], HIGHEST)
    SC[...] = scores
    heads = lax.broadcasted_iota(jnp.int32, (1, T), 1)
    channels = lax.broadcasted_iota(jnp.int32, (1, 256), 1) // 64

    def by_lane(ref, lanes):
        out = jnp.zeros(lanes.shape, F32)
        for h in range(4):
            out = jnp.where(lanes == h, ref[0, h], out)
        return out

    STEP[...] = jnp.zeros((T, T), F32)
    STEP[0:4, :] = stepin_ref[...].astype(F32)
    raw = STEP[...].T + by_lane(bias_ref, heads)
    SIG[...] = jax.nn.sigmoid(raw)
    step = jnp.maximum(raw, 0.0) + jnp.log1p(jnp.exp(-jnp.abs(raw)))
    rate = -jnp.exp(by_lane(decay_ref, heads))
    SK[0:1, 0:128] = rate
    run_col = nn(causal.astype(F32), step * rate, HIGHEST)
    run_row = run_col.T
    stepl = nn(step, rep, HIGHEST)
    STL[...] = stepl
    skipl = by_lane(skip_ref, channels)
    SK[1:2] = skipl
    scaled = mix * stepl
    low = ci < 64
    ys = []
    for pair in range(2):
        sp = scaled[:, pair * 128 : pair * 128 + 128]
        acc = None
        for half in range(2):
            h = pair * 2 + half
            differ = run_col[:, h : h + 1] - run_row[h : h + 1, :]
            em = jnp.where(causal, jnp.exp(jnp.where(causal, differ, 0.0)), 0.0)
            EM[h] = em
            w = em * scores
            WTC[pair, :, half * 128 : half * 128 + 128] = w.T.astype(BF16)
            keep = low if half == 0 else jnp.logical_not(low)
            sh = jnp.where(keep, sp, 0.0)
            SCM[h] = sh.astype(BF16)
            part = nn(w, sh, HIGHEST)
            acc = part if acc is None else acc + part
        ys.append(acc)
    y = jnp.concatenate(ys, axis=1) + skipl * mix
    sg = jax.nn.sigmoid(gate)
    silu_gate = gate * sg
    gated = y * silu_gate
    inverse = lax.rsqrt(jnp.sum(gated * gated, axis=1, keepdims=True) * (1.0 / 256.0) + EPSILON)
    NRM[...] = gated * inverse
    SGI[...] = silu_gate * inverse
    YSP[...] = y * (sg * (1.0 + gate * (1.0 - sg))) * inverse

    ks = (0, 1, 3, 2)

    def spread(src_j, dst_j, target, h, k):
        return remote(G.at[c, k, src_j, pieces[h]], G.at[c, k, dst_j, pieces[h]], target)

    grid = [(h, k) for h in range(H) for k in ks]
    to_r = {hk: spread(0, 3, to_right, *hk) for hk in grid}
    to_l = {hk: spread(0, 1, to_left, *hk) for hk in grid}
    to_o = {hk: spread(0, 2, to_opposite, *hk) for hk in grid}
    to_m = {
        (h, k): remote(G.at[c, k, :, pieces[h]], G.at[c, k, :, pieces[h]], mate) for h, k in grid
    }

    loads[16].wait()

    @pl.when(early)
    def _():
        turn(0, 32)

    @pl.when(jnp.logical_and(early, inner))
    def _():
        relay(range(4))

    @pl.when(jnp.logical_and(early, jnp.logical_not(inner)))
    def _():
        accept()

    for h, k in grid:
        first[h][FAR.index((4 - k) % 4)].wait_recv()
        go(to_o[h, k])
        go(to_r[h, k])
        go(to_l[h, k])

    @pl.when(jnp.logical_and(s == 3, inner))
    def _():
        relay((0, 1))

    @pl.when(s == 3)
    def _():
        turn(0, 24)

    for i in range(16):
        loads[i].wait()

    def multiply(k):
        lefts, rights = [], []
        for h in range(H):
            to_m[h, k].wait_recv()
        for j in range(4):
            lefts += [G[0, k, j], G[1, k, j]]
            rights.append(WO[((x + j) % NX) * NZ + (z + k) % NZ])
        part = nt(jnp.concatenate(lefts, axis=1), jnp.concatenate(rights, axis=1))
        return part if k == ks[0] else ACC[...] + part

    for n, (h, k) in enumerate(grid):
        to_o[h, k].wait_recv()
        to_r[h, k].wait_recv()
        to_l[h, k].wait_recv()
        go(to_m[h, k])
        if n == 2 * H - 1:

            @pl.when(jnp.logical_and(s == 3, inner))
            def _():
                relay((2,))

        if h == H - 1 and k != ks[0]:
            before = ks[ks.index(k) - 1]
            ACC[...] = multiply(before)

    @pl.when(s == 3)
    def _():
        turn(24, 32)

    @pl.when(jnp.logical_and(s == 3, inner))
    def _():
        relay((3,))

    acc = multiply(ks[3])

    dn = acc * gain_ref[...]
    nrm = NRM[...]
    mu = jnp.sum(dn * nrm, axis=1, keepdims=True) * (1.0 / 256.0)
    e = dn - nrm * mu
    dy = e * SGI[...]
    L[:, 0:256] = (e * YSP[...]).astype(BF16)
    dyb = dy.astype(BF16)
    ds = None
    masks = []
    for h in range(4):
        a = nt(dyb[:, h // 2 * 128 : h // 2 * 128 + 128], SCM[h]) * EM[h]
        ds = a if ds is None else ds + a
        masks.append((a * SC[...]).astype(BF16))
    db = nn(ds.T.astype(BF16), BC[:, 128:256])
    dc = nn(ds.astype(BF16), BC[:, 0:128])
    dstate = jnp.concatenate([db, dc], axis=1) * DSS[...]
    L[:, 512:768] = conv_back(dstate, CS[...], rows).astype(BF16)
    dscs = []
    for pair in range(2):
        dyp = dyb[:, pair * 128 : pair * 128 + 128]
        zero = jnp.zeros_like(dyp)
        both = jnp.concatenate([jnp.where(low, dyp, zero), jnp.where(low, zero, dyp)], axis=0)
        dscs.append(nn(WTC[pair], both))
    dscaled = jnp.concatenate(dscs, axis=1)
    dmix = (dscaled * STL[...] + SK[1:2] * dy) * DSM[...]
    L[:, 256:512] = conv_back(dmix, cm_ref[...], rows).astype(BF16)
    upper = (ci >= ri).astype(BF16)
    sums = nn(upper, jnp.concatenate(masks, axis=1))
    before = jnp.concatenate([ci < ri] * 4, axis=1)
    sums = jnp.where(before, sums, 0.0).astype(BF16)
    pick = (
        lax.broadcasted_iota(jnp.int32, (512, T), 0) // 128
        == lax.broadcasted_iota(jnp.int32, (512, T), 1)
    ).astype(BF16)
    ddecay = nn(sums, pick)
    pick64 = (
        lax.broadcasted_iota(jnp.int32, (256, T), 0) // 64
        == lax.broadcasted_iota(jnp.int32, (256, T), 1)
    ).astype(BF16)
    dstep = nn((dscaled * MIX[...]).astype(BF16), pick64)
    dstep = dstep + ddecay * SK[0:1, 0:128]
    L[:, 768:896] = (dstep * SIG[...]).astype(BF16)

    @pl.when(jnp.logical_and(s == 3, jnp.logical_not(inner)))
    def _():
        accept()

    for load in loads[17:]:
        load.wait()
    for copy in mine + shares:
        copy.wait_recv()
    lhs = L[...]
    first_core = c == 0
    to_mate = {}

    def input_block(j, k):
        index = ((x + j) % NX) * NZ + (z + FAR[k]) % NZ
        at = pl.ds(pl.multiple_of(index * 256, 256), 256)
        part = nn(lhs, W[:, at])
        lower, upper_half = part[:, 0:128], part[:, 128:256]
        Q[j, k] = jnp.where(first_core, lower, upper_half)
        PS[k, j] = jnp.where(first_core, upper_half, lower).astype(BF16)

    arrived = set()

    def chip_sum(j, k, h):
        if k not in arrived:
            arrived.add(k)
            to_mate[k].wait_recv()
        return Q[j, k, pieces[h]] + PR[k, j, pieces[h]].astype(F32)

    sends = {}
    zcopies = {}
    totals = {}
    sides = ((2, to_opposite), (1, to_right), (3, to_left))

    def send_x(h, k):
        for n, (j, target) in enumerate(sides):
            XS[n, k, pieces[h]] = chip_sum(j, k, h).astype(BF16)
            sends[n, h, k] = go(remote(XS.at[n, k, pieces[h]], XR.at[n, k, pieces[h]], target))

    def send_z(h, k):
        value = chip_sum(0, k, h)
        for n in (1, 2, 0):
            sends[n, h, k].wait_recv()
            value = value + XR[n, k, pieces[h]].astype(F32)
        if k < 3:
            ZS[k, pieces[h]] = value.astype(BF16)
            zcopies[h, k] = go(
                remote(
                    ZS.at[k, pieces[h]], ZR.at[k, pieces[h]],
                    dev(place(x, (z + FAR[k]) % NZ, c)),
                )
            )
        else:
            totals[h] = value

    for k in range(5):
        if k < 4:
            for j in FAR:
                input_block(j, k)
            to_mate[k] = go(remote(PS.at[k], PR.at[k], mate))
        if k > 0:
            for h in range(H):
                send_x(h, k - 1)
    for h in range(H):
        for k in range(4):
            send_z(h, k)
    for h in range(H):
        total = totals[h]
        for k in (1, 2, 0):
            zcopies[h, k].wait_recv()
            total = total + ZR[k, pieces[h]].astype(F32)
        out_ref[pieces[h], :] = total.astype(BF16)
        last = hand_off(out_ref, h)

        @pl.when(s > 0)
        def _():
            for copy in last:
                copy.start()

    for copies in first:
        for copy in copies:
            copy.wait_send()
    for copy in pending + shares:
        copy.wait_send()

    @pl.when(inner)
    def _():
        for copy in swaps + passes:
            copy.wait_send()


N_COPIES = H * (4 + 12 + 4 + 12 + 3) + 4 + 16


def body(
    weight_main, weight_state, weight_step, weight_out, conv_main, conv_state, step_bias,
    decay_log, skip_gain, norm_gain, saved_main, saved_state, saved_step, output_grad,
):
    ws = jnp.transpose(weight_state[0], (1, 2, 0))
    vmem = pl.BlockSpec(memory_space=pltpu.VMEM)
    hbm = pl.BlockSpec(memory_space=pltpu.HBM)
    block = (T, T)
    wide = (T, 256)
    result = pl.pallas_call(
        kernel,
        out_shape=jax.ShapeDtypeStruct((T, T), BF16),
        in_specs=[hbm] * 14,
        out_specs=vmem,
        scratch_shapes=[
            pltpu.SMEM((1, 4), F32),
            pltpu.SMEM((1, 4), F32),
            pltpu.SMEM((1, 4), F32),
            pltpu.VMEM((4, 4096), BF16),
            pltpu.VMEM((T, 2, 256), BF16),
            pltpu.VMEM((T, 2, 128), BF16),
            pltpu.VMEM((4, T), BF16),
            pltpu.VMEM((4, 256), F32),
            pltpu.VMEM((4, 2, 128), F32),
            pltpu.VMEM((1, 256), F32),
            pltpu.VMEM((4096, 2, 256), BF16),
            pltpu.VMEM((896, 4096), BF16),
            pltpu.VMEM((16, 256, 256), BF16),
            pltpu.VMEM(block, F32),
            pltpu.VMEM((2, 4, 4) + block, BF16),
            pltpu.VMEM((4, 4) + block, F32),
            pltpu.VMEM((4, 4) + block, BF16),
            pltpu.VMEM((4, 4) + block, BF16),
            pltpu.VMEM((3, 4) + block, BF16),
            pltpu.VMEM((3, 4) + block, BF16),
            pltpu.VMEM((3,) + block, BF16),
            pltpu.VMEM((3,) + block, BF16),
            pltpu.VMEM(wide, F32),
            pltpu.VMEM(wide, F32),
            pltpu.VMEM(wide, F32),
            pltpu.VMEM(wide, F32),
            pltpu.VMEM(wide, F32),
            pltpu.VMEM(wide, F32),
            pltpu.VMEM(wide, F32),
            pltpu.VMEM((4,) + block, F32),
            pltpu.VMEM(block, F32),
            pltpu.VMEM((2, T, 256), BF16),
            pltpu.VMEM((4,) + block, BF16),
            pltpu.VMEM(wide, BF16),
            pltpu.VMEM(block, F32),
            pltpu.VMEM((8, 256), F32),
            pltpu.VMEM((4, 256), F32),
            pltpu.VMEM((T, 896), BF16),
            pltpu.VMEM(wide, F32),
            pltpu.SemaphoreType.DMA((31,)),
            pltpu.SemaphoreType.DMA((N_COPIES,)),
            pltpu.SemaphoreType.DMA((N_COPIES,)),
        ],
        compiler_params=pltpu.CompilerParams(
            collective_id=0, has_side_effects=True, vmem_limit_bytes=67043328
        ),
        name="relay",
    )(
        weight_main[0], ws, weight_out[0], step_bias, decay_log, skip_gain, weight_step[0],
        saved_main[0], saved_state[0], saved_step[0], conv_main[0], conv_state[0], norm_gain,
        output_grad,
    )
    return result[None]


def solution(mesh):
    return jax.shard_map(
        body,
        mesh=mesh,
        in_specs=(
            P("pipe", None, None, "tensor"),
            P("pipe", None, None, "tensor"),
            P("pipe", "tensor", None),
            P("pipe", "tensor", None),
            P("pipe", None, "tensor"),
            P("pipe", None, None, None),
            P("pipe", "tensor"),
            P("pipe", "tensor"),
            P("pipe", "tensor"),
            P("pipe", "tensor"),
            P("pipe", "dp", None, "tensor"),
            P("pipe", "dp", None, None),
            P("pipe", "tensor", "dp"),
            P("dp", "tensor"),
        ),
        out_specs=P("pipe", "dp", "tensor"),
        check_vma=False,
    )
```

```python
import jax
import jax.numpy as jnp
from jax import lax
from jax.experimental import pallas as pl
from jax.experimental.pallas import tpu as pltpu
from jax.sharding import PartitionSpec as P

F32 = jnp.float32
BF16 = jnp.bfloat16
HIGHEST = lax.Precision.HIGHEST
EPSILON = 1e-05
MESH = pl.DeviceIdType.MESH
NX = 4
NZ = 4
T = 128
FAR = (2, 1, 3, 0)
H = 2
TH = T // H


def nn(a, b, precision=None):
    return lax.dot_general(
        a, b, (((1,), (0,)), ((), ())), preferred_element_type=F32, precision=precision
    )


def nt(a, b, precision=None):
    return lax.dot_general(
        a, b, (((1,), (1,)), ((), ())), preferred_element_type=F32, precision=precision
    )


def shift_down(v, n, rows):
    if n == 0:
        return v
    return jnp.where(rows >= n, pltpu.roll(v, n, 0), 0.0)


def shift_up(v, n, rows):
    if n == 0:
        return v
    return jnp.where(rows < T - n, pltpu.roll(v, T - n, 0), 0.0)


def conv(v, taps, rows):
    out = taps[3:4] * v
    for k in range(3):
        out = out + taps[k : k + 1] * shift_down(v, 3 - k, rows)
    return out


def conv_back(v, taps, rows):
    out = taps[3:4] * v
    for k in range(3):
        out = out + taps[k : k + 1] * shift_up(v, 3 - k, rows)
    return out


def kernel(
    wm_hbm, ws_hbm, wo_hbm,
    bias_hbm, decay_hbm, skip_hbm,
    wt_hbm, main_hbm, state_hbm, stepin_hbm, cm_hbm, cs_hbm, gain_hbm, og_hbm,
    out_ref,
    bias_ref, decay_ref, skip_ref, wt_ref, main_ref, state_ref, stepin_ref, cm_ref, cs_ref, gain_ref,
    RAW, W, WO, STEP, G, Q, PS, PR, XS, XR, ZS, ZR,
    NRM, SGI, YSP, MIX, STL, DSM, DSS, EM, SC, WTC, SCM, BC, SIG, SK, CS, L, ACC,
    wsem, ssem, rsem,
):
    s = lax.axis_index("pipe")
    t = lax.axis_index("tensor")
    x = t // 8
    z = (t // 2) % 4
    c = t % 2
    d = lax.axis_index("dp")
    right_x = (x + 1) % NX
    left_x = (x + 3) % NX
    below = (s + 3) % 4
    above = (s + 1) % 4

    def place(px, pz, pc):
        return (px * NZ + pz) * 2 + pc

    def dev(tt, ss=None):
        if ss is None:
            return {"tensor": tt}
        return {"pipe": ss, "tensor": tt}

    count = [0]
    pending = []

    def remote(src, dst, target):
        i = count[0]
        count[0] += 1
        return pltpu.make_async_remote_copy(
            src_ref=src, dst_ref=dst, send_sem=ssem.at[i], recv_sem=rsem.at[i],
            device_id=target, device_id_type=MESH,
        )

    def go(copy):
        copy.start()
        pending.append(copy)
        return copy

    mate = dev(place(x, z, 1 - c))
    to_right = dev(place(right_x, z, c))
    to_left = dev(place(left_x, z, c))
    to_opposite = dev(place((x + 2) % NX, z, c))
    pair_z = z + 1 - 2 * (z % 2)
    inner = z % 2 != d
    to_inner = {"tensor": place(x, pair_z, c), "dp": 1 - d}
    to_outer = {"tensor": t, "dp": 1 - d}

    barrier = pltpu.get_barrier_semaphore()
    partners = [mate, to_right, to_left, to_opposite, to_inner, to_outer]
    for o in (1, 2, 3):
        partners.append(dev(place(x, (z + o) % NZ, c)))
    for o in range(4):
        partners.append(dev(place(x, (z + o) % NZ, c), below))
        partners.append(dev(place(x, (z + o) % NZ, c), above))
    for p in partners:
        pl.semaphore_signal(barrier, inc=1, device_id=p, device_id_type=MESH)

    group = pl.ds(pl.multiple_of(t // 4 * 128, 128), 128)
    small = [
        (main_hbm, main_ref), (state_hbm.at[:, :, group], state_ref), (cm_hbm, cm_ref),
        (cs_hbm.at[:, :, group], cs_ref), (stepin_hbm, stepin_ref), (bias_hbm, bias_ref),
        (decay_hbm, decay_ref), (skip_hbm, skip_ref), (gain_hbm, gain_ref), (wt_hbm, wt_ref),
    ]
    small = [pltpu.make_async_copy(src, dst, wsem.at[21 + i]) for i, (src, dst) in enumerate(small)]
    for load in small:
        load.start()
    loads = [
        pltpu.make_async_copy(wo_hbm.at[:, pl.ds(i * 256, 256)], WO.at[i], wsem.at[i])
        for i in range(16)
    ]
    loads.append(pltpu.make_async_copy(wm_hbm, RAW, wsem.at[16]))
    m = t % 4
    cuts = [(half, pl.ds(part * 2048, 2048)) for half in range(2) for part in range(2)]

    def columns(member, half, lanes):
        return W.at[pl.ds(pl.multiple_of(512 + half * 128 + member * 32, 32), 32), lanes]

    def own_columns(half, lanes):
        return ws_hbm.at[half, :, lanes]

    loads += [
        pltpu.make_async_copy(own_columns(*cut), columns(m, *cut), wsem.at[17 + q])
        for q, cut in enumerate(cuts)
    ]
    for load in loads:
        load.start()

    pl.semaphore_wait(barrier, len(partners))

    pieces = [pl.ds(h * TH, TH) for h in range(H)]
    hand_ids = list(range(count[0], count[0] + 4 * H))
    count[0] += 4 * H

    def hand_off(block, h):
        copies = []
        for n, o in enumerate(FAR):
            i = hand_ids[4 * h + n]
            copies.append(
                pltpu.make_async_remote_copy(
                    src_ref=block.at[pieces[h]], dst_ref=G.at[c, (4 - o) % 4, 0, pieces[h]],
                    send_sem=ssem.at[i], recv_sem=rsem.at[i],
                    device_id=dev(place(x, (z + o) % NZ, c), below), device_id_type=MESH,
                )
            )
        return copies

    first = [hand_off(og_hbm, h) for h in range(H)]

    @pl.when(s == 0)
    def _():
        for copies in first:
            for copy in copies:
                copy.start()

    mine = [go(remote(own_columns(*cut), columns(m, *cut), mate)) for cut in cuts]
    swaps = [remote(own_columns(*cut), columns(m, *cut), to_inner) for cut in cuts]
    other = (m + 2) % 4
    passes = [remote(columns(other, *cut), columns(other, *cut), to_outer) for cut in cuts]
    shares = [remote(columns(other, *cut), columns(other, *cut), mate) for cut in cuts]

    @pl.when(inner)
    def _():
        for copy in swaps:
            copy.start()

    def relay(chosen):
        for q in chosen:
            swaps[q].wait_recv()
            passes[q].start()
            shares[q].start()

    def accept():
        for q in range(4):
            passes[q].wait_recv()
            shares[q].start()

    early = s != 3
    for load in small:
        load.wait()
    W[768:896, :] = jnp.zeros((128, 4096), BF16)
    W[768:772, :] = wt_ref[...]

    apart_row = lax.broadcasted_iota(jnp.int32, (256, 256), 0)
    apart_col = lax.broadcasted_iota(jnp.int32, (256, 256), 1)
    apart = (apart_col == 2 * (apart_row % 128) + apart_row // 128).astype(BF16)

    def turn(first_block, last_block):
        def one(i, carry):
            at = pl.ds(pl.multiple_of(i * 128, 128), 128)
            both = lax.dot_general(
                RAW[at].reshape(256, 256), apart, (((0,), (1,)), ((), ())),
                preferred_element_type=F32,
            ).astype(BF16)
            W[0:256, at] = both[:, 0:128]
            W[256:512, at] = both[:, 128:256]
            return carry

        lax.fori_loop(first_block, last_block, one, 0, unroll=4)

    rows = lax.broadcasted_iota(jnp.int32, (T, 256), 0)
    ri = lax.broadcasted_iota(jnp.int32, (T, T), 0)
    ci = lax.broadcasted_iota(jnp.int32, (T, T), 1)
    causal = ri >= ci
    rep = (
        lax.broadcasted_iota(jnp.int32, (T, 256), 0)
        == lax.broadcasted_iota(jnp.int32, (T, 256), 1) // 64
    ).astype(F32)
    pair_in = nn(apart, main_ref[...].reshape(256, 256))
    gate = pair_in[0:128]
    cm = cm_ref[...]
    cs = jnp.concatenate([cs_ref[:, 0, :], cs_ref[:, 1, :]], axis=1)
    CS[...] = cs
    mixed = conv(pair_in[128:256], cm, rows)
    sig = jax.nn.sigmoid(mixed)
    mix = mixed * sig
    DSM[...] = sig * (1.0 + mixed * (1.0 - sig))
    MIX[...] = mix
    pair_in = nn(apart, state_ref[...].reshape(256, 128))
    states = conv(jnp.concatenate([pair_in[0:128], pair_in[128:256]], axis=1), cs, rows)
    sig = jax.nn.sigmoid(states)
    DSS[...] = sig * (1.0 + states * (1.0 - sig))
    states = states * sig
    BC[...] = states.astype(BF16)
    scores = nt(states[:, 128:256], states[:, 0:128], HIGHEST)
    SC[...] = scores
    heads = lax.broadcasted_iota(jnp.int32, (1, T), 1)
    channels = lax.broadcasted_iota(jnp.int32, (1, 256), 1) // 64

    def by_lane(ref, lanes):
        out = jnp.zeros(lanes.shape, F32)
        for h in range(4):
            out = jnp.where(lanes == h, ref[0, h], out)
        return out

    STEP[...] = jnp.zeros((T, T), F32)
    STEP[0:4, :] = stepin_ref[...].astype(F32)
    raw = STEP[...].T + by_lane(bias_ref, heads)
    SIG[...] = jax.nn.sigmoid(raw)
    step = jnp.maximum(raw, 0.0) + jnp.log1p(jnp.exp(-jnp.abs(raw)))
    rate = -jnp.exp(by_lane(decay_ref, heads))
    SK[0:1, 0:128] = rate
    run_col = nn(causal.astype(F32), step * rate, HIGHEST)
    run_row = run_col.T
    stepl = nn(step, rep, HIGHEST)
    STL[...] = stepl
    skipl = by_lane(skip_ref, channels)
    SK[1:2] = skipl
    scaled = mix * stepl
    low = ci < 64
    ys = []
    for pair in range(2):
        sp = scaled[:, pair * 128 : pair * 128 + 128]
        acc = None
        for half in range(2):
            h = pair * 2 + half
            differ = run_col[:, h : h + 1] - run_row[h : h + 1, :]
            em = jnp.where(causal, jnp.exp(jnp.where(causal, differ, 0.0)), 0.0)
            EM[h] = em
            w = em * scores
            WTC[pair, :, half * 128 : half * 128 + 128] = w.T.astype(BF16)
            keep = low if half == 0 else jnp.logical_not(low)
            sh = jnp.where(keep, sp, 0.0)
            SCM[h] = sh.astype(BF16)
            part = nn(w, sh, HIGHEST)
            acc = part if acc is None else acc + part
        ys.append(acc)
    y = jnp.concatenate(ys, axis=1) + skipl * mix
    sg = jax.nn.sigmoid(gate)
    silu_gate = gate * sg
    gated = y * silu_gate
    inverse = lax.rsqrt(jnp.sum(gated * gated, axis=1, keepdims=True) * (1.0 / 256.0) + EPSILON)
    NRM[...] = gated * inverse
    SGI[...] = silu_gate * inverse
    YSP[...] = y * (sg * (1.0 + gate * (1.0 - sg))) * inverse

    ks = (0, 1, 3, 2)

    def spread(src_j, dst_j, target, h, k):
        return remote(G.at[c, k, src_j, pieces[h]], G.at[c, k, dst_j, pieces[h]], target)

    grid = [(h, k) for h in range(H) for k in ks]
    to_r = {hk: spread(0, 3, to_right, *hk) for hk in grid}
    to_l = {hk: spread(0, 1, to_left, *hk) for hk in grid}
    to_o = {hk: spread(0, 2, to_opposite, *hk) for hk in grid}
    to_m = {
        (h, k): remote(G.at[c, k, :, pieces[h]], G.at[c, k, :, pieces[h]], mate) for h, k in grid
    }

    loads[16].wait()

    @pl.when(early)
    def _():
        turn(0, 32)

    @pl.when(jnp.logical_and(early, inner))
    def _():
        relay(range(4))

    @pl.when(jnp.logical_and(early, jnp.logical_not(inner)))
    def _():
        accept()

    for h, k in grid:
        first[h][FAR.index((4 - k) % 4)].wait_recv()
        go(to_o[h, k])
        go(to_r[h, k])
        go(to_l[h, k])

    @pl.when(jnp.logical_and(s == 3, inner))
    def _():
        relay((0, 1))

    @pl.when(s == 3)
    def _():
        turn(0, 24)

    for i in range(16):
        loads[i].wait()

    def multiply(k):
        lefts, rights = [], []
        for h in range(H):
            to_m[h, k].wait_recv()
        for j in range(4):
            lefts += [G[0, k, j], G[1, k, j]]
            rights.append(WO[((x + j) % NX) * NZ + (z + k) % NZ])
        part = nt(jnp.concatenate(lefts, axis=1), jnp.concatenate(rights, axis=1))
        return part if k == ks[0] else ACC[...] + part

    for n, (h, k) in enumerate(grid):
        to_o[h, k].wait_recv()
        to_r[h, k].wait_recv()
        to_l[h, k].wait_recv()
        go(to_m[h, k])
        if n == 2 * H - 1:

            @pl.when(jnp.logical_and(s == 3, inner))
            def _():
                relay((2,))

        if h == H - 1 and k != ks[0]:
            before = ks[ks.index(k) - 1]
            ACC[...] = multiply(before)

    @pl.when(s == 3)
    def _():
        turn(24, 32)

    @pl.when(jnp.logical_and(s == 3, inner))
    def _():
        relay((3,))

    acc = multiply(ks[3])

    dn = acc * gain_ref[...]
    nrm = NRM[...]
    mu = jnp.sum(dn * nrm, axis=1, keepdims=True) * (1.0 / 256.0)
    e = dn - nrm * mu
    dy = e * SGI[...]
    L[:, 0:256] = (e * YSP[...]).astype(BF16)
    dyb = dy.astype(BF16)
    ds = None
    masks = []
    for h in range(4):
        a = nt(dyb[:, h // 2 * 128 : h // 2 * 128 + 128], SCM[h]) * EM[h]
        ds = a if ds is None else ds + a
        masks.append((a * SC[...]).astype(BF16))
    db = nn(ds.T.astype(BF16), BC[:, 128:256])
    dc = nn(ds.astype(BF16), BC[:, 0:128])
    dstate = jnp.concatenate([db, dc], axis=1) * DSS[...]
    L[:, 512:768] = conv_back(dstate, CS[...], rows).astype(BF16)
    dscs = []
    for pair in range(2):
        dyp = dyb[:, pair * 128 : pair * 128 + 128]
        zero = jnp.zeros_like(dyp)
        both = jnp.concatenate([jnp.where(low, dyp, zero), jnp.where(low, zero, dyp)], axis=0)
        dscs.append(nn(WTC[pair], both))
    dscaled = jnp.concatenate(dscs, axis=1)
    dmix = (dscaled * STL[...] + SK[1:2] * dy) * DSM[...]
    L[:, 256:512] = conv_back(dmix, cm_ref[...], rows).astype(BF16)
    upper = (ci >= ri).astype(BF16)
    sums = nn(upper, jnp.concatenate(masks, axis=1))
    before = jnp.concatenate([ci < ri] * 4, axis=1)
    sums = jnp.where(before, sums, 0.0).astype(BF16)
    pick = (
        lax.broadcasted_iota(jnp.int32, (512, T), 0) // 128
        == lax.broadcasted_iota(jnp.int32, (512, T), 1)
    ).astype(BF16)
    ddecay = nn(sums, pick)
    pick64 = (
        lax.broadcasted_iota(jnp.int32, (256, T), 0) // 64
        == lax.broadcasted_iota(jnp.int32, (256, T), 1)
    ).astype(BF16)
    dstep = nn((dscaled * MIX[...]).astype(BF16), pick64)
    dstep = dstep + ddecay * SK[0:1, 0:128]
    L[:, 768:896] = (dstep * SIG[...]).astype(BF16)

    @pl.when(jnp.logical_and(s == 3, jnp.logical_not(inner)))
    def _():
        accept()

    for load in loads[17:]:
        load.wait()
    for copy in mine + shares:
        copy.wait_recv()
    lhs = L[...]
    first_core = c == 0
    to_mate = {}

    def input_block(j, k):
        index = ((x + j) % NX) * NZ + (z + FAR[k]) % NZ
        at = pl.ds(pl.multiple_of(index * 256, 256), 256)
        part = nn(lhs, W[:, at])
        lower, upper_half = part[:, 0:128], part[:, 128:256]
        Q[j, k] = jnp.where(first_core, lower, upper_half)
        PS[k, j] = jnp.where(first_core, upper_half, lower).astype(BF16)

    arrived = set()

    def chip_sum(j, k, h):
        if k not in arrived:
            arrived.add(k)
            to_mate[k].wait_recv()
        return Q[j, k, pieces[h]] + PR[k, j, pieces[h]].astype(F32)

    sends = {}
    zcopies = {}
    totals = {}
    sides = ((2, to_opposite), (1, to_right), (3, to_left))

    def send_x(h, k):
        for n, (j, target) in enumerate(sides):
            XS[n, k, pieces[h]] = chip_sum(j, k, h).astype(BF16)
            sends[n, h, k] = go(remote(XS.at[n, k, pieces[h]], XR.at[n, k, pieces[h]], target))

    def send_z(h, k):
        value = chip_sum(0, k, h)
        for n in (1, 2, 0):
            sends[n, h, k].wait_recv()
            value = value + XR[n, k, pieces[h]].astype(F32)
        if k < 3:
            ZS[k, pieces[h]] = value.astype(BF16)
            zcopies[h, k] = go(
                remote(
                    ZS.at[k, pieces[h]], ZR.at[k, pieces[h]],
                    dev(place(x, (z + FAR[k]) % NZ, c)),
                )
            )
        else:
            totals[h] = value

    for k in range(5):
        if k < 4:
            for j in FAR:
                input_block(j, k)
            to_mate[k] = go(remote(PS.at[k], PR.at[k], mate))
        if k > 0:
            send_x(0, k - 1)
    for h in range(1, H):
        for k in range(4):
            send_x(h, k)
    for h in range(H):
        for k in range(4):
            send_z(h, k)
    for h in range(H):
        total = totals[h]
        for k in (1, 2, 0):
            zcopies[h, k].wait_recv()
            total = total + ZR[k, pieces[h]].astype(F32)
        out_ref[pieces[h], :] = total.astype(BF16)
        last = hand_off(out_ref, h)

        @pl.when(s > 0)
        def _():
            for copy in last:
                copy.start()

    for copies in first:
        for copy in copies:
            copy.wait_send()
    for copy in pending + shares:
        copy.wait_send()

    @pl.when(inner)
    def _():
        for copy in swaps + passes:
            copy.wait_send()


N_COPIES = H * (4 + 12 + 4 + 12 + 3) + 4 + 16


def body(
    weight_main, weight_state, weight_step, weight_out, conv_main, conv_state, step_bias,
    decay_log, skip_gain, norm_gain, saved_main, saved_state, saved_step, output_grad,
):
    ws = jnp.transpose(weight_state[0], (1, 2, 0))
    vmem = pl.BlockSpec(memory_space=pltpu.VMEM)
    hbm = pl.BlockSpec(memory_space=pltpu.HBM)
    block = (T, T)
    wide = (T, 256)
    result = pl.pallas_call(
        kernel,
        out_shape=jax.ShapeDtypeStruct((T, T), BF16),
        in_specs=[hbm] * 14,
        out_specs=vmem,
        scratch_shapes=[
            pltpu.SMEM((1, 4), F32),
            pltpu.SMEM((1, 4), F32),
            pltpu.SMEM((1, 4), F32),
            pltpu.VMEM((4, 4096), BF16),
            pltpu.VMEM((T, 2, 256), BF16),
            pltpu.VMEM((T, 2, 128), BF16),
            pltpu.VMEM((4, T), BF16),
            pltpu.VMEM((4, 256), F32),
            pltpu.VMEM((4, 2, 128), F32),
            pltpu.VMEM((1, 256), F32),
            pltpu.VMEM((4096, 2, 256), BF16),
            pltpu.VMEM((896, 4096), BF16),
            pltpu.VMEM((16, 256, 256), BF16),
            pltpu.VMEM(block, F32),
            pltpu.VMEM((2, 4, 4) + block, BF16),
            pltpu.VMEM((4, 4) + block, F32),
            pltpu.VMEM((4, 4) + block, BF16),
            pltpu.VMEM((4, 4) + block, BF16),
            pltpu.VMEM((3, 4) + block, BF16),
            pltpu.VMEM((3, 4) + block, BF16),
            pltpu.VMEM((3,) + block, BF16),
            pltpu.VMEM((3,) + block, BF16),
            pltpu.VMEM(wide, F32),
            pltpu.VMEM(wide, F32),
            pltpu.VMEM(wide, F32),
            pltpu.VMEM(wide, F32),
            pltpu.VMEM(wide, F32),
            pltpu.VMEM(wide, F32),
            pltpu.VMEM(wide, F32),
            pltpu.VMEM((4,) + block, F32),
            pltpu.VMEM(block, F32),
            pltpu.VMEM((2, T, 256), BF16),
            pltpu.VMEM((4,) + block, BF16),
            pltpu.VMEM(wide, BF16),
            pltpu.VMEM(block, F32),
            pltpu.VMEM((8, 256), F32),
            pltpu.VMEM((4, 256), F32),
            pltpu.VMEM((T, 896), BF16),
            pltpu.VMEM(wide, F32),
            pltpu.SemaphoreType.DMA((31,)),
            pltpu.SemaphoreType.DMA((N_COPIES,)),
            pltpu.SemaphoreType.DMA((N_COPIES,)),
        ],
        compiler_params=pltpu.CompilerParams(
            collective_id=0, has_side_effects=True, vmem_limit_bytes=67043328
        ),
        name="relay",
    )(
        weight_main[0], ws, weight_out[0], step_bias, decay_log, skip_gain, weight_step[0],
        saved_main[0], saved_state[0], saved_step[0], conv_main[0], conv_state[0], norm_gain,
        output_grad,
    )
    return result[None]


def solution(mesh):
    return jax.shard_map(
        body,
        mesh=mesh,
        in_specs=(
            P("pipe", None, None, "tensor"),
            P("pipe", None, None, "tensor"),
            P("pipe", "tensor", None),
            P("pipe", "tensor", None),
            P("pipe", None, "tensor"),
            P("pipe", None, None, None),
            P("pipe", "tensor"),
            P("pipe", "tensor"),
            P("pipe", "tensor"),
            P("pipe", "tensor"),
            P("pipe", "dp", None, "tensor"),
            P("pipe", "dp", None, None),
            P("pipe", "tensor", "dp"),
            P("dp", "tensor"),
        ),
        out_specs=P("pipe", "dp", "tensor"),
        check_vma=False,
    )
```

```python
import jax
import jax.numpy as jnp
from jax import lax
from jax.experimental import pallas as pl
from jax.experimental.pallas import tpu as pltpu
from jax.sharding import PartitionSpec as P

F32 = jnp.float32
BF16 = jnp.bfloat16
HIGHEST = lax.Precision.HIGHEST
EPSILON = 1e-05
MESH = pl.DeviceIdType.MESH
NX = 4
NZ = 4
T = 128
FAR = (2, 1, 3, 0)
H = 2
TH = T // H


def nn(a, b, precision=None):
    return lax.dot_general(
        a, b, (((1,), (0,)), ((), ())), preferred_element_type=F32, precision=precision
    )


def nt(a, b, precision=None):
    return lax.dot_general(
        a, b, (((1,), (1,)), ((), ())), preferred_element_type=F32, precision=precision
    )


def shift_down(v, n, rows):
    if n == 0:
        return v
    return jnp.where(rows >= n, pltpu.roll(v, n, 0), 0.0)


def shift_up(v, n, rows):
    if n == 0:
        return v
    return jnp.where(rows < T - n, pltpu.roll(v, T - n, 0), 0.0)


def conv(v, taps, rows):
    out = taps[3:4] * v
    for k in range(3):
        out = out + taps[k : k + 1] * shift_down(v, 3 - k, rows)
    return out


def conv_back(v, taps, rows):
    out = taps[3:4] * v
    for k in range(3):
        out = out + taps[k : k + 1] * shift_up(v, 3 - k, rows)
    return out


def kernel(
    wm_hbm, ws_hbm, wo_hbm,
    bias_hbm, decay_hbm, skip_hbm,
    wt_hbm, main_hbm, state_hbm, stepin_hbm, cm_hbm, cs_hbm, gain_hbm, og_hbm,
    out_ref,
    bias_ref, decay_ref, skip_ref, wt_ref, main_ref, state_ref, stepin_ref, cm_ref, cs_ref, gain_ref,
    RAW, W, WO, STEP, G, Q, PS, PR, XS, XR, ZS, ZR,
    NRM, SGI, YSP, MIX, STL, DSM, DSS, EM, SC, WTC, SCM, BC, SIG, SK, CS, L, ACC,
    wsem, ssem, rsem,
):
    s = lax.axis_index("pipe")
    t = lax.axis_index("tensor")
    x = t // 8
    z = (t // 2) % 4
    c = t % 2
    d = lax.axis_index("dp")
    right_x = (x + 1) % NX
    left_x = (x + 3) % NX
    below = (s + 3) % 4
    above = (s + 1) % 4

    def place(px, pz, pc):
        return (px * NZ + pz) * 2 + pc

    def dev(tt, ss=None):
        if ss is None:
            return {"tensor": tt}
        return {"pipe": ss, "tensor": tt}

    count = [0]
    pending = []

    def remote(src, dst, target):
        i = count[0]
        count[0] += 1
        return pltpu.make_async_remote_copy(
            src_ref=src, dst_ref=dst, send_sem=ssem.at[i], recv_sem=rsem.at[i],
            device_id=target, device_id_type=MESH,
        )

    def go(copy):
        copy.start()
        pending.append(copy)
        return copy

    mate = dev(place(x, z, 1 - c))
    to_right = dev(place(right_x, z, c))
    to_left = dev(place(left_x, z, c))
    to_opposite = dev(place((x + 2) % NX, z, c))
    pair_z = z + 1 - 2 * (z % 2)
    inner = z % 2 != d
    to_inner = {"tensor": place(x, pair_z, c), "dp": 1 - d}
    to_outer = {"tensor": t, "dp": 1 - d}

    barrier = pltpu.get_barrier_semaphore()
    partners = [mate, to_right, to_left, to_opposite, to_inner, to_outer]
    for o in (1, 2, 3):
        partners.append(dev(place(x, (z + o) % NZ, c)))
    for o in range(4):
        partners.append(dev(place(x, (z + o) % NZ, c), below))
        partners.append(dev(place(x, (z + o) % NZ, c), above))
    for p in partners:
        pl.semaphore_signal(barrier, inc=1, device_id=p, device_id_type=MESH)

    group = pl.ds(pl.multiple_of(t // 4 * 128, 128), 128)
    small = [
        (main_hbm, main_ref), (state_hbm.at[:, :, group], state_ref), (cm_hbm, cm_ref),
        (cs_hbm.at[:, :, group], cs_ref), (stepin_hbm, stepin_ref), (bias_hbm, bias_ref),
        (decay_hbm, decay_ref), (skip_hbm, skip_ref), (gain_hbm, gain_ref), (wt_hbm, wt_ref),
    ]
    small = [pltpu.make_async_copy(src, dst, wsem.at[21 + i]) for i, (src, dst) in enumerate(small)]
    for load in small:
        load.start()
    loads = [
        pltpu.make_async_copy(wo_hbm.at[:, pl.ds(i * 256, 256)], WO.at[i], wsem.at[i])
        for i in range(16)
    ]
    loads.append(pltpu.make_async_copy(wm_hbm, RAW, wsem.at[16]))
    m = t % 4
    cuts = [(half, pl.ds(part * 2048, 2048)) for half in range(2) for part in range(2)]

    def columns(member, half, lanes):
        return W.at[pl.ds(pl.multiple_of(512 + half * 128 + member * 32, 32), 32), lanes]

    def own_columns(half, lanes):
        return ws_hbm.at[half, :, lanes]

    loads += [
        pltpu.make_async_copy(own_columns(*cut), columns(m, *cut), wsem.at[17 + q])
        for q, cut in enumerate(cuts)
    ]
    for load in loads:
        load.start()

    pl.semaphore_wait(barrier, len(partners))

    pieces = [pl.ds(h * TH, TH) for h in range(H)]
    hand_ids = list(range(count[0], count[0] + 4 * H))
    count[0] += 4 * H

    def hand_off(block, h):
        copies = []
        for n, o in enumerate(FAR):
            i = hand_ids[4 * h + n]
            copies.append(
                pltpu.make_async_remote_copy(
                    src_ref=block.at[pieces[h]], dst_ref=G.at[c, (4 - o) % 4, 0, pieces[h]],
                    send_sem=ssem.at[i], recv_sem=rsem.at[i],
                    device_id=dev(place(x, (z + o) % NZ, c), below), device_id_type=MESH,
                )
            )
        return copies

    first = [hand_off(og_hbm, h) for h in range(H)]

    @pl.when(s == 0)
    def _():
        for copies in first:
            for copy in copies:
                copy.start()

    mine = [go(remote(own_columns(*cut), columns(m, *cut), mate)) for cut in cuts]
    swaps = [remote(own_columns(*cut), columns(m, *cut), to_inner) for cut in cuts]
    other = (m + 2) % 4
    passes = [remote(columns(other, *cut), columns(other, *cut), to_outer) for cut in cuts]
    shares = [remote(columns(other, *cut), columns(other, *cut), mate) for cut in cuts]

    @pl.when(inner)
    def _():
        for copy in swaps:
            copy.start()

    def relay(chosen):
        for q in chosen:
            swaps[q].wait_recv()
            passes[q].start()
            shares[q].start()

    def accept(chosen):
        for q in chosen:
            passes[q].wait_recv()
            shares[q].start()

    early = s != 3
    for load in small:
        load.wait()
    W[768:896, :] = jnp.zeros((128, 4096), BF16)
    W[768:772, :] = wt_ref[...]

    apart_row = lax.broadcasted_iota(jnp.int32, (256, 256), 0)
    apart_col = lax.broadcasted_iota(jnp.int32, (256, 256), 1)
    apart = (apart_col == 2 * (apart_row % 128) + apart_row // 128).astype(BF16)

    def turn(first_block, last_block):
        def one(i, carry):
            at = pl.ds(pl.multiple_of(i * 128, 128), 128)
            both = lax.dot_general(
                RAW[at].reshape(256, 256), apart, (((0,), (1,)), ((), ())),
                preferred_element_type=F32,
            ).astype(BF16)
            W[0:256, at] = both[:, 0:128]
            W[256:512, at] = both[:, 128:256]
            return carry

        lax.fori_loop(first_block, last_block, one, 0, unroll=4)

    rows = lax.broadcasted_iota(jnp.int32, (T, 256), 0)
    ri = lax.broadcasted_iota(jnp.int32, (T, T), 0)
    ci = lax.broadcasted_iota(jnp.int32, (T, T), 1)
    causal = ri >= ci
    rep = (
        lax.broadcasted_iota(jnp.int32, (T, 256), 0)
        == lax.broadcasted_iota(jnp.int32, (T, 256), 1) // 64
    ).astype(F32)
    pair_in = nn(apart, main_ref[...].reshape(256, 256))
    gate = pair_in[0:128]
    cm = cm_ref[...]
    cs = jnp.concatenate([cs_ref[:, 0, :], cs_ref[:, 1, :]], axis=1)
    CS[...] = cs
    mixed = conv(pair_in[128:256], cm, rows)
    sig = jax.nn.sigmoid(mixed)
    mix = mixed * sig
    DSM[...] = sig * (1.0 + mixed * (1.0 - sig))
    MIX[...] = mix
    pair_in = nn(apart, state_ref[...].reshape(256, 128))
    states = conv(jnp.concatenate([pair_in[0:128], pair_in[128:256]], axis=1), cs, rows)
    sig = jax.nn.sigmoid(states)
    DSS[...] = sig * (1.0 + states * (1.0 - sig))
    states = states * sig
    BC[...] = states.astype(BF16)
    scores = nt(states[:, 128:256], states[:, 0:128], HIGHEST)
    SC[...] = scores
    heads = lax.broadcasted_iota(jnp.int32, (1, T), 1)
    channels = lax.broadcasted_iota(jnp.int32, (1, 256), 1) // 64

    def by_lane(ref, lanes):
        out = jnp.zeros(lanes.shape, F32)
        for h in range(4):
            out = jnp.where(lanes == h, ref[0, h], out)
        return out

    STEP[...] = jnp.zeros((T, T), F32)
    STEP[0:4, :] = stepin_ref[...].astype(F32)
    raw = STEP[...].T + by_lane(bias_ref, heads)
    SIG[...] = jax.nn.sigmoid(raw)
    step = jnp.maximum(raw, 0.0) + jnp.log1p(jnp.exp(-jnp.abs(raw)))
    rate = -jnp.exp(by_lane(decay_ref, heads))
    SK[0:1, 0:128] = rate
    run_col = nn(causal.astype(F32), step * rate, HIGHEST)
    run_row = run_col.T
    stepl = nn(step, rep, HIGHEST)
    STL[...] = stepl
    skipl = by_lane(skip_ref, channels)
    SK[1:2] = skipl
    scaled = mix * stepl
    low = ci < 64
    ys = []
    for pair in range(2):
        sp = scaled[:, pair * 128 : pair * 128 + 128]
        acc = None
        for half in range(2):
            h = pair * 2 + half
            differ = run_col[:, h : h + 1] - run_row[h : h + 1, :]
            em = jnp.where(causal, jnp.exp(jnp.where(causal, differ, 0.0)), 0.0)
            EM[h] = em
            w = em * scores
            WTC[pair, :, half * 128 : half * 128 + 128] = w.T.astype(BF16)
            keep = low if half == 0 else jnp.logical_not(low)
            sh = jnp.where(keep, sp, 0.0)
            SCM[h] = sh.astype(BF16)
            part = nn(w, sh, HIGHEST)
            acc = part if acc is None else acc + part
        ys.append(acc)
    y = jnp.concatenate(ys, axis=1) + skipl * mix
    sg = jax.nn.sigmoid(gate)
    silu_gate = gate * sg
    gated = y * silu_gate
    inverse = lax.rsqrt(jnp.sum(gated * gated, axis=1, keepdims=True) * (1.0 / 256.0) + EPSILON)
    NRM[...] = gated * inverse
    SGI[...] = silu_gate * inverse
    YSP[...] = y * (sg * (1.0 + gate * (1.0 - sg))) * inverse

    ks = (0, 1, 3, 2)

    def spread(src_j, dst_j, target, h, k):
        return remote(G.at[c, k, src_j, pieces[h]], G.at[c, k, dst_j, pieces[h]], target)

    grid = [(h, k) for h in range(H) for k in ks]
    to_r = {hk: spread(0, 3, to_right, *hk) for hk in grid}
    to_l = {hk: spread(0, 1, to_left, *hk) for hk in grid}
    to_o = {hk: spread(0, 2, to_opposite, *hk) for hk in grid}
    to_m = {
        (h, k): remote(G.at[c, k, :, pieces[h]], G.at[c, k, :, pieces[h]], mate) for h, k in grid
    }

    loads[16].wait()

    @pl.when(early)
    def _():
        turn(0, 32)

    @pl.when(jnp.logical_and(early, inner))
    def _():
        relay(range(4))

    @pl.when(jnp.logical_and(early, jnp.logical_not(inner)))
    def _():
        accept(range(4))

    for h, k in grid:
        first[h][FAR.index((4 - k) % 4)].wait_recv()
        go(to_o[h, k])
        go(to_r[h, k])
        go(to_l[h, k])

    @pl.when(jnp.logical_and(s == 3, inner))
    def _():
        relay((0, 1))

    @pl.when(s == 3)
    def _():
        turn(0, 24)

    for i in range(16):
        loads[i].wait()

    def multiply(k):
        lefts, rights = [], []
        for h in range(H):
            to_m[h, k].wait_recv()
        for j in range(4):
            lefts += [G[0, k, j], G[1, k, j]]
            rights.append(WO[((x + j) % NX) * NZ + (z + k) % NZ])
        part = nt(jnp.concatenate(lefts, axis=1), jnp.concatenate(rights, axis=1))
        return part if k == ks[0] else ACC[...] + part

    for n, (h, k) in enumerate(grid):
        to_o[h, k].wait_recv()
        to_r[h, k].wait_recv()
        to_l[h, k].wait_recv()
        go(to_m[h, k])
        if n in (1, 5):

            @pl.when(jnp.logical_and(s == 3, inner))
            def _():
                relay((2,) if n == 1 else (3,))

        if h == H - 1 and k != ks[0]:
            before = ks[ks.index(k) - 1]
            ACC[...] = multiply(before)

    @pl.when(s == 3)
    def _():
        turn(24, 32)

    @pl.when(jnp.logical_and(s == 3, jnp.logical_not(inner)))
    def _():
        accept((0, 1))

    acc = multiply(ks[3])

    dn = acc * gain_ref[...]
    nrm = NRM[...]
    mu = jnp.sum(dn * nrm, axis=1, keepdims=True) * (1.0 / 256.0)
    e = dn - nrm * mu
    dy = e * SGI[...]
    L[:, 0:256] = (e * YSP[...]).astype(BF16)
    dyb = dy.astype(BF16)
    ds = None
    masks = []
    for h in range(4):
        a = nt(dyb[:, h // 2 * 128 : h // 2 * 128 + 128], SCM[h]) * EM[h]
        ds = a if ds is None else ds + a
        masks.append((a * SC[...]).astype(BF16))
    db = nn(ds.T.astype(BF16), BC[:, 128:256])
    dc = nn(ds.astype(BF16), BC[:, 0:128])
    dstate = jnp.concatenate([db, dc], axis=1) * DSS[...]
    L[:, 512:768] = conv_back(dstate, CS[...], rows).astype(BF16)
    dscs = []
    for pair in range(2):
        dyp = dyb[:, pair * 128 : pair * 128 + 128]
        zero = jnp.zeros_like(dyp)
        both = jnp.concatenate([jnp.where(low, dyp, zero), jnp.where(low, zero, dyp)], axis=0)
        dscs.append(nn(WTC[pair], both))
    dscaled = jnp.concatenate(dscs, axis=1)
    dmix = (dscaled * STL[...] + SK[1:2] * dy) * DSM[...]
    L[:, 256:512] = conv_back(dmix, cm_ref[...], rows).astype(BF16)
    upper = (ci >= ri).astype(BF16)
    sums = nn(upper, jnp.concatenate(masks, axis=1))
    before = jnp.concatenate([ci < ri] * 4, axis=1)
    sums = jnp.where(before, sums, 0.0).astype(BF16)
    pick = (
        lax.broadcasted_iota(jnp.int32, (512, T), 0) // 128
        == lax.broadcasted_iota(jnp.int32, (512, T), 1)
    ).astype(BF16)
    ddecay = nn(sums, pick)
    pick64 = (
        lax.broadcasted_iota(jnp.int32, (256, T), 0) // 64
        == lax.broadcasted_iota(jnp.int32, (256, T), 1)
    ).astype(BF16)
    dstep = nn((dscaled * MIX[...]).astype(BF16), pick64)
    dstep = dstep + ddecay * SK[0:1, 0:128]
    L[:, 768:896] = (dstep * SIG[...]).astype(BF16)

    @pl.when(jnp.logical_and(s == 3, jnp.logical_not(inner)))
    def _():
        accept((2, 3))

    for load in loads[17:]:
        load.wait()
    for copy in mine + shares:
        copy.wait_recv()
    lhs = L[...]
    first_core = c == 0
    to_mate = {}

    def input_block(j, k):
        index = ((x + j) % NX) * NZ + (z + FAR[k]) % NZ
        at = pl.ds(pl.multiple_of(index * 256, 256), 256)
        part = nn(lhs, W[:, at])
        lower, upper_half = part[:, 0:128], part[:, 128:256]
        Q[j, k] = jnp.where(first_core, lower, upper_half)
        PS[k, j] = jnp.where(first_core, upper_half, lower).astype(BF16)

    arrived = set()

    def chip_sum(j, k, h):
        if k not in arrived:
            arrived.add(k)
            to_mate[k].wait_recv()
        return Q[j, k, pieces[h]] + PR[k, j, pieces[h]].astype(F32)

    sends = {}
    zcopies = {}
    totals = {}
    sides = ((2, to_opposite), (1, to_right), (3, to_left))

    def send_x(h, k):
        for n, (j, target) in enumerate(sides):
            XS[n, k, pieces[h]] = chip_sum(j, k, h).astype(BF16)
            sends[n, h, k] = go(remote(XS.at[n, k, pieces[h]], XR.at[n, k, pieces[h]], target))

    def send_z(h, k):
        value = chip_sum(0, k, h)
        for n in (1, 2, 0):
            sends[n, h, k].wait_recv()
            value = value + XR[n, k, pieces[h]].astype(F32)
        if k < 3:
            ZS[k, pieces[h]] = value.astype(BF16)
            zcopies[h, k] = go(
                remote(
                    ZS.at[k, pieces[h]], ZR.at[k, pieces[h]],
                    dev(place(x, (z + FAR[k]) % NZ, c)),
                )
            )
        else:
            totals[h] = value

    for k in range(5):
        if k < 4:
            for j in FAR:
                input_block(j, k)
            to_mate[k] = go(remote(PS.at[k], PR.at[k], mate))
        if k > 0:
            send_x(0, k - 1)
    for h in range(1, H):
        for k in range(4):
            send_x(h, k)
    for h in range(H):
        for k in range(4):
            send_z(h, k)
    for h in range(H):
        total = totals[h]
        for k in (1, 2, 0):
            zcopies[h, k].wait_recv()
            total = total + ZR[k, pieces[h]].astype(F32)
        out_ref[pieces[h], :] = total.astype(BF16)
        last = hand_off(out_ref, h)

        @pl.when(s > 0)
        def _():
            for copy in last:
                copy.start()

    for copies in first:
        for copy in copies:
            copy.wait_send()
    for copy in pending + shares:
        copy.wait_send()

    @pl.when(inner)
    def _():
        for copy in swaps + passes:
            copy.wait_send()


N_COPIES = H * (4 + 12 + 4 + 12 + 3) + 4 + 16


def body(
    weight_main, weight_state, weight_step, weight_out, conv_main, conv_state, step_bias,
    decay_log, skip_gain, norm_gain, saved_main, saved_state, saved_step, output_grad,
):
    ws = jnp.transpose(weight_state[0], (1, 2, 0))
    vmem = pl.BlockSpec(memory_space=pltpu.VMEM)
    hbm = pl.BlockSpec(memory_space=pltpu.HBM)
    block = (T, T)
    wide = (T, 256)
    result = pl.pallas_call(
        kernel,
        out_shape=jax.ShapeDtypeStruct((T, T), BF16),
        in_specs=[hbm] * 14,
        out_specs=vmem,
        scratch_shapes=[
            pltpu.SMEM((1, 4), F32),
            pltpu.SMEM((1, 4), F32),
            pltpu.SMEM((1, 4), F32),
            pltpu.VMEM((4, 4096), BF16),
            pltpu.VMEM((T, 2, 256), BF16),
            pltpu.VMEM((T, 2, 128), BF16),
            pltpu.VMEM((4, T), BF16),
            pltpu.VMEM((4, 256), F32),
            pltpu.VMEM((4, 2, 128), F32),
            pltpu.VMEM((1, 256), F32),
            pltpu.VMEM((4096, 2, 256), BF16),
            pltpu.VMEM((896, 4096), BF16),
            pltpu.VMEM((16, 256, 256), BF16),
            pltpu.VMEM(block, F32),
            pltpu.VMEM((2, 4, 4) + block, BF16),
            pltpu.VMEM((4, 4) + block, F32),
            pltpu.VMEM((4, 4) + block, BF16),
            pltpu.VMEM((4, 4) + block, BF16),
            pltpu.VMEM((3, 4) + block, BF16),
            pltpu.VMEM((3, 4) + block, BF16),
            pltpu.VMEM((3,) + block, BF16),
            pltpu.VMEM((3,) + block, BF16),
            pltpu.VMEM(wide, F32),
            pltpu.VMEM(wide, F32),
            pltpu.VMEM(wide, F32),
            pltpu.VMEM(wide, F32),
            pltpu.VMEM(wide, F32),
            pltpu.VMEM(wide, F32),
            pltpu.VMEM(wide, F32),
            pltpu.VMEM((4,) + block, F32),
            pltpu.VMEM(block, F32),
            pltpu.VMEM((2, T, 256), BF16),
            pltpu.VMEM((4,) + block, BF16),
            pltpu.VMEM(wide, BF16),
            pltpu.VMEM(block, F32),
            pltpu.VMEM((8, 256), F32),
            pltpu.VMEM((4, 256), F32),
            pltpu.VMEM((T, 896), BF16),
            pltpu.VMEM(wide, F32),
            pltpu.SemaphoreType.DMA((31,)),
            pltpu.SemaphoreType.DMA((N_COPIES,)),
            pltpu.SemaphoreType.DMA((N_COPIES,)),
        ],
        compiler_params=pltpu.CompilerParams(
            collective_id=0, has_side_effects=True, vmem_limit_bytes=67043328
        ),
        name="relay",
    )(
        weight_main[0], ws, weight_out[0], step_bias, decay_log, skip_gain, weight_step[0],
        saved_main[0], saved_state[0], saved_step[0], conv_main[0], conv_state[0], norm_gain,
        output_grad,
    )
    return result[None]


def solution(mesh):
    return jax.shard_map(
        body,
        mesh=mesh,
        in_specs=(
            P("pipe", None, None, "tensor"),
            P("pipe", None, None, "tensor"),
            P("pipe", "tensor", None),
            P("pipe", "tensor", None),
            P("pipe", None, "tensor"),
            P("pipe", None, None, None),
            P("pipe", "tensor"),
            P("pipe", "tensor"),
            P("pipe", "tensor"),
            P("pipe", "tensor"),
            P("pipe", "dp", None, "tensor"),
            P("pipe", "dp", None, None),
            P("pipe", "tensor", "dp"),
            P("dp", "tensor"),
        ),
        out_specs=P("pipe", "dp", "tensor"),
        check_vma=False,
    )
```
